32 devices in a mesh: groups: 2 (over x), utt: 16 (over z, y, core).
Axes of the slice: x: 2, y: 2, z: 4, core: 2. Of those that a mesh axis runs over, the one named last changes fastest.
Arguments:
- cache_kv: bfloat16 [512, 8, 3072], P(('groups', 'utt')), parts along dimension 0, may hold values from -160 to 160
- new_rows: bfloat16 [512, 4608], P(('groups', 'utt')), parts along dimension 0, may hold values from -6 to 6
- cross_queries: bfloat16 [512, 1536], P(('groups', 'utt')), parts along dimension 0, may hold values from -6 to 6
- enc_kv: bfloat16 [32, 256, 3072], P(('groups', 'utt')), parts along dimension 0, may hold values from -160 to 160
- lengths: int32 [32], P(('groups', 'utt')), parts along dimension 0, may hold values from 64 to 256, as said below
- parents: int32 [32, 16], P(('groups', 'utt')), parts along dimension 0, may hold values from 0 to 15
Outputs:
- mixed: bfloat16 [512, 1536], P(('groups', 'utt')), parts along dimension 0
The draws below stay inside these ranges and needn't reach their ends.
There are 2 independent parts, one for each index of `groups`. The reference program is written for one: setup_inputs(seed, part) draws one part's arguments, and reference() takes and returns one part's arrays. A program takes and returns all parts, laid end to end along the dimension named above; each array names one. Nothing has to cross between parts.
Inputs may be any that keep to these rules, and one draw needn't show every extreme that they name: `lengths`: some utterance of each part has all 256 frames.
All inputs are finite; a program needn't handle non-finite values.
Results may differ from the reference program's by a relative error of at most 0.009.
Values may be sent and summed in bfloat16 or wider, within the bound.
A program may use at most 64 MiB of HBM per device.

```python
import jax
import jax.numpy as jnp
from jax import lax

BEAM = 16
HEADS = 12
HD = 128
PREV = 8
FRAMES = 256
FEAT = 1536
ULOC = 1
UTT = 16
HYP = 256
N_UTT = 16


def draw_cache_kv(key, part):
    shape = (HYP, PREV, 2 * FEAT)
    drawn = jax.random.truncated_normal(key, -8.0, 8.0, shape, jnp.float32)
    return drawn.astype(jnp.bfloat16)


def draw_enc_kv(key, part):
    shape = (UTT, FRAMES, 2 * FEAT)
    drawn = jax.random.truncated_normal(key, -8.0, 8.0, shape, jnp.float32)
    return drawn.astype(jnp.bfloat16)


def draw_lengths(key, part):
    spans = jax.random.randint(key, (UTT,), FRAMES // 4, FRAMES + 1)
    longest = jax.random.randint(jax.random.fold_in(key, 17), (), 0, UTT)
    places = lax.broadcasted_iota(jnp.int32, (UTT,), 0)
    return jnp.where(places == longest, FRAMES, spans).astype(jnp.int32)


def set_ends(values, rng, smallest, high):
    shape = values.shape
    spot = [jax.random.randint(jax.random.fold_in(rng, axis), (), 0, shape[axis]) for axis in range(len(shape))]
    values = values.at[tuple(spot)].set(smallest)
    longest = shape.index(max(shape))
    spot[longest] = (spot[longest] + 1) % shape[longest]
    return values.at[tuple(spot)].set(high)


def shard_levels(stream_key, shape, shards, low, high):
    gain = 1.0
    for axis_at, parts in shards:
        draws = jax.random.uniform(jax.random.fold_in(jax.random.fold_in(stream_key, 6), axis_at), (parts,), jnp.float32, low / len(shards), high / len(shards))
        gain = gain * jnp.repeat(jnp.exp(draws), shape[axis_at] // parts).reshape((-1,) + (1,) * (len(shape) - 1 - axis_at))
    return gain


def bell_draw(rng, shape, spread, bound, shards=(), held_as=jnp.bfloat16):
    entries = jax.random.normal(rng, shape, jnp.float32) * spread
    if len(shards) > 0:
        entries = shard_levels(rng, shape, shards, -0.22, 0.18) * entries
    return jnp.clip(entries, min=-bound, max=bound).astype(held_as)


def setup_inputs(seed: int = 0, part: int = 0) -> dict:
    splits = jax.random.split(jax.random.key(seed), 7)
    own_keys = jax.random.split(jax.random.fold_in(splits[6], part), 7)
    cache_kv = draw_cache_kv(jax.random.fold_in(jax.random.fold_in(splits[6], part), 71), part)
    new_rows = bell_draw(own_keys[1], (HYP, 3 * FEAT), 1.0, 6.0, ((0, 16),))
    cross_queries = bell_draw(own_keys[2], (HYP, FEAT), 1.0, 6.0, ((0, 16),))
    enc_kv = draw_enc_kv(jax.random.fold_in(jax.random.fold_in(splits[6], part), 71), part)
    lengths = draw_lengths(jax.random.fold_in(jax.random.fold_in(splits[6], part), 71), part)
    parents = set_ends(jax.random.randint(own_keys[5], (UTT, BEAM), 0, BEAM), jax.random.fold_in(own_keys[5], 1), 0, BEAM - 1).astype(jnp.int32)
    return {"cache_kv": cache_kv, "new_rows": new_rows, "cross_queries": cross_queries, "enc_kv": enc_kv, "lengths": lengths, "parents": parents}


def to_utterance(lm_rows):
    rest = lm_rows.shape[1:]
    grouped = lm_rows.reshape((ULOC, BEAM, N_UTT) + rest)
    order = (2, 0, 1) + tuple(range(3, 3 + len(rest)))
    return jnp.transpose(grouped, order).reshape((ULOC * BEAM * N_UTT,) + rest)


def to_grouped(utt_rows):
    width = utt_rows.shape[1]
    grouped = utt_rows.reshape(N_UTT, ULOC, BEAM, width)
    return jnp.transpose(grouped, (1, 2, 0, 3)).reshape(HYP, width)


def attend_self(query, old_keys, old_values, new_key, new_value):
    row_count = query.shape[0]
    history = old_keys.shape[1]
    scale = HD ** -0.5
    query_heads = query.astype(jnp.float32).reshape(row_count, HEADS, HD)
    key_heads = old_keys.astype(jnp.float32).reshape(row_count, history, HEADS, HD)
    value_heads = old_values.astype(jnp.float32).reshape(row_count, history, HEADS, HD)
    old_scores = jnp.einsum("rhd,rthd->rht", query_heads, key_heads) * scale
    own_score = jnp.einsum("rhd,rhd->rh", query_heads, new_key.astype(jnp.float32).reshape(row_count, HEADS, HD)) * scale
    peak = jnp.maximum(jnp.max(old_scores, axis=2), own_score)
    old_exp = jnp.exp(old_scores - peak[:, :, None])
    own_exp = jnp.exp(own_score - peak)
    total = jnp.sum(old_exp, axis=2) + own_exp
    old_weight = (old_exp / total[:, :, None]).astype(jnp.bfloat16).astype(jnp.float32)
    own_weight = (own_exp / total).astype(jnp.bfloat16).astype(jnp.float32)
    context = jnp.einsum("rht,rthd->rhd", old_weight, value_heads)
    context = context + own_weight[:, :, None] * new_value.astype(jnp.float32).reshape(row_count, HEADS, HD)
    return context.reshape(row_count, HEADS * HD).astype(jnp.bfloat16)


def attend_frames(queries, frames_kv, frame_counts):
    utterances = frame_counts.shape[0]
    frame_total = frames_kv.shape[1]
    scale = HD ** -0.5
    query_heads = queries.astype(jnp.float32).reshape(utterances, BEAM, HEADS, HD)
    key_heads = frames_kv[:, :, :FEAT].astype(jnp.float32).reshape(utterances, frame_total, HEADS, HD)
    value_heads = frames_kv[:, :, FEAT:].astype(jnp.float32).reshape(utterances, frame_total, HEADS, HD)
    scores = jnp.einsum("ubhd,ufhd->uhbf", query_heads, key_heads) * scale
    live = lax.broadcasted_iota(jnp.int32, (utterances, 1, 1, frame_total), 3) < frame_counts[:, None, None, None]
    scores = jnp.where(live, scores, -1e30)
    peak = jnp.max(scores, axis=3, keepdims=True)
    raised = jnp.where(live, jnp.exp(scores - peak), 0.0)
    weights = (raised / jnp.sum(raised, axis=3, keepdims=True)).astype(jnp.bfloat16).astype(jnp.float32)
    context = jnp.einsum("uhbf,ufhd->ubhd", weights, value_heads)
    return context.reshape(utterances * BEAM, HEADS * HD)


def reference(cache_kv, new_rows, cross_queries, enc_kv, lengths, parents):
    cache_u = to_utterance(cache_kv)
    new_u = to_utterance(new_rows)
    grouped = cache_u.reshape(UTT, BEAM, PREV, 2 * FEAT)
    reordered = jax.vmap(lambda block, picks: block[picks])(grouped, parents).reshape(HYP, PREV, 2 * FEAT)
    self_context = attend_self(new_u[:, :FEAT], reordered[:, :, :FEAT], reordered[:, :, FEAT:], new_u[:, FEAT:2 * FEAT], new_u[:, 2 * FEAT:])
    cross_context = attend_frames(cross_queries, enc_kv, lengths)
    mixed_u = (self_context.astype(jnp.float32) + cross_context).astype(jnp.bfloat16)
    return to_grouped(mixed_u)
```

```python
import functools

import jax
import jax.numpy as jnp
from jax import lax
from jax.experimental import pallas as pl
from jax.experimental.pallas import tpu as pltpu
from jax.sharding import PartitionSpec as P

HD = 128
CORES = 2
LINES = 2
PARTS = 3


def chunk_sizes(heads):
    first = heads // 3
    return [first, heads - first] if first else [heads]
LOW = -1e30


def contract_last(a, b):
    return lax.dot_general(a, b, (((1,), (1,)), ((), ())), preferred_element_type=jnp.float32)


def fast_kernel(
    n,
    cache_ref, new_ref, cq_ref, enc_ref, len_ref, par_ref,
    out_ref,
    qbuf, kbuf, vbuf, newbuf, cqbuf, encbuf, ptab, ctx, ybuf, sbuf, zbuf, xsend, xrecv,
    local_sem, q_send, q_recv, f_send, c_send, c_recv, p_send, p_recv, x_send, x_recv,
    y_send, y_recv, z_send, z_recv, qown_sem, stay_sem, len_smem,
):
    feature = cq_ref.shape[1]
    half = feature // CORES
    heads = half // HD
    sizes = chunk_sizes(heads)
    chunks = len(sizes)
    starts = [sum(sizes[:k]) for k in range(chunks)]
    rows = cq_ref.shape[0]
    utts = new_ref.shape[0]
    old = cache_ref.shape[0]
    history = old // utts
    depth = n // (CORES * LINES)
    scale = HD ** (-0.5)

    me = lax.axis_index("utt")
    z = me // (CORES * LINES)
    y = (me // CORES) % LINES
    c = me % CORES
    y_other = 1 - y
    c_other = 1 - c

    def at(zz, yy, cc):
        return (zz * LINES + yy) * CORES + cc

    def remote(src, dst, ssem, rsem, dev):
        return pltpu.make_async_remote_copy(
            src_ref=src, dst_ref=dst, send_sem=ssem, recv_sem=rsem,
            device_id={"utt": dev}, device_id_type=pl.DeviceIdType.MESH,
        )

    barrier = pltpu.get_barrier_semaphore()
    for k in range(1, n):
        pl.semaphore_signal(
            barrier, inc=1, device_id={"utt": lax.rem(me + k, n)},
            device_id_type=pl.DeviceIdType.MESH,
        )

    def chunk_cols(cc, k):
        return pl.ds(pl.multiple_of(cc * half + starts[k] * HD, HD), sizes[k] * HD)

    my_half = pl.ds(pl.multiple_of(c * half, HD), half)
    my_values = pl.ds(pl.multiple_of(feature + c * half, HD), half)
    my_rows = pl.ds(pl.multiple_of(c * old, old), old)
    copies = [
        pltpu.make_async_copy(cq_ref, cqbuf, local_sem.at[0]),
        pltpu.make_async_copy(enc_ref.at[0], encbuf, local_sem.at[1]),
        pltpu.make_async_copy(new_ref, newbuf, local_sem.at[2]),
        pltpu.make_async_copy(cache_ref.at[:, my_half], kbuf.at[my_rows], local_sem.at[4]),
        pltpu.make_async_copy(cache_ref.at[:, my_values], vbuf.at[my_rows], local_sem.at[5]),
        pltpu.make_async_copy(par_ref, ptab.at[me], local_sem.at[6]),
    ] + [
        pltpu.make_async_copy(new_ref.at[:, chunk_cols(c, k)], qbuf[k].at[z, y, c], qown_sem.at[k])
        for k in range(chunks)
    ]
    get_len = pltpu.make_async_copy(len_ref, len_smem, local_sem.at[3])
    get_len.start()
    for cp in copies:
        cp.start()

    get_len.wait()
    copies[0].wait()
    copies[1].wait()

    frames = encbuf.shape[0]
    live = lax.broadcasted_iota(jnp.int32, (rows, frames), 1) < len_smem[0]
    ones_f = jnp.ones((frames, HD), jnp.bfloat16)

    def cross(h):
        cols = slice(h * HD, (h + 1) * HD)
        s = contract_last(cqbuf[:, cols], encbuf[:, cols]) * scale
        s = jnp.where(live, s, LOW)
        p = jnp.where(live, jnp.exp(s - jnp.max(s, axis=1, keepdims=True)), 0.0).astype(jnp.bfloat16)
        v = jnp.concatenate([encbuf[:, feature + h * HD : feature + (h + 1) * HD], ones_f], axis=1)
        o = jnp.dot(p, v, preferred_element_type=jnp.float32)
        o = o[:, :HD] / o[:, HD:]
        for b in range(rows):
            xsend[b, :, cols] = o[b : b + 1, :]

    early = (feature // HD) // 3
    for h in range(early):
        cross(h)

    copies[2].wait()
    pl.semaphore_wait(barrier, n - 1)

    sends = []

    def spread(k):
        slot = 0
        for dz in (*range(1, depth), 0):
            zz = lax.rem(z + dz, depth)
            for dc in range(CORES):
                cc = lax.rem(c + dc, CORES)
                for yy in (y_other, y) if dz == 0 else (y,):
                    if dz == 0 and dc == 0 and yy is y:
                        continue
                    cp = remote(newbuf.at[:, chunk_cols(cc, k)], qbuf[k].at[z, y, c],
                                q_send.at[k, slot], q_recv.at[k, me], at(zz, yy, cc))
                    cp.start()
                    sends.append(cp)
                    slot += 1

    spread(0)
    for k in range(1, n):
        dev = lax.rem(me + k, n)
        cp = remote(par_ref, ptab.at[me], p_send.at[k - 1], p_recv.at[me], dev)
        cp.start()
        sends.append(cp)
    for k in range(1, chunks):
        spread(k)
    other_half = pl.ds(pl.multiple_of(c_other * half, HD), half)
    other_values = pl.ds(pl.multiple_of(feature + c_other * half, HD), half)
    partner = at(z, y, c_other)
    cache_in = []
    for i, (cols, buf) in enumerate(((other_half, kbuf), (other_values, vbuf))):
        cp = remote(cache_ref.at[:, cols], buf.at[my_rows], c_send.at[i], c_recv.at[i], partner)
        cp.start()
        sends.append(cp)
        cache_in.append(cp)

    def forward(k):
        slot = 0
        for dz in range(1, depth):
            zz = lax.rem(z + dz, depth)
            for cc in range(CORES):
                src = at(zz, y, cc)
                piece = qbuf[k].at[zz, y, cc]
                remote(piece, piece, f_send.at[k, slot], q_recv.at[k, src], src).wait_recv()
                cp = remote(piece, piece, f_send.at[k, slot], q_recv.at[k, src], at(z, y_other, c))
                cp.start()
                sends.append(cp)
                slot += 1

    forward(0)

    for h in range(early, feature // HD):
        cross(h)

    own_x = pltpu.make_async_copy(xsend.at[me], xrecv.at[me], local_sem.at[7])
    own_x.start()
    copies[3].wait()
    copies[4].wait()
    for cp in cache_in:
        cp.wait_recv()
    copies[5].wait()
    for k in range(1, n):
        src = lax.rem(me + n - k, n)
        remote(par_ref, ptab.at[src], p_send.at[0], p_recv.at[src], src).wait_recv()

    table = jnp.concatenate([ptab[u] for u in range(utts)], axis=0)
    beam_lane = lax.broadcasted_iota(jnp.int32, table.shape, 1)
    row_u = lax.broadcasted_iota(jnp.int32, (utts, 1), 0)
    chip = me // CORES
    keys = CORES * old
    ones_k = jnp.ones((keys, HD), jnp.bfloat16)

    def masks(yy):
        target = []
        for zz in range(depth):
            for cc in range(CORES):
                col = jnp.sum(jnp.where(beam_lane == at(zz, yy, cc), table, 0), axis=1, keepdims=True)
                target.append((col - chip * CORES) * utts + row_u)
        target = jnp.concatenate(target, axis=0)
        valid = lax.broadcasted_iota(jnp.int32, (count, keys), 1) // history == target
        sel = jnp.broadcast_to((target >= 0) & (target < CORES * utts), (count, HD))
        return valid, sel

    count = depth * CORES * utts
    lane = lax.broadcasted_iota(jnp.int32, (count, HD), 1)

    def partial(yy, mask, stats, k):
        valid, sel = mask
        for hk in range(sizes[k]):
            h = starts[k] + hk
            cols = slice(h * HD, (h + 1) * HD)
            kcols = slice(hk * HD, (hk + 1) * HD)
            q = qbuf[k][:, pl.ds(yy, 1), :, :, kcols].reshape(count, HD)
            s = jnp.where(valid, contract_last(q, kbuf[:, cols]) * scale, LOW)
            m = jnp.max(s, axis=1, keepdims=True)
            p = jnp.where(valid, jnp.exp(s - m), 0.0).astype(jnp.bfloat16)
            v = jnp.concatenate([vbuf[:, cols], ones_k], axis=1)
            o = jnp.dot(p, v, preferred_element_type=jnp.float32)
            total = jnp.where(sel, o[:, HD:], 1.0)
            ctx[k][:, pl.ds(yy, 1), :, :, kcols] = (o[:, :HD] / total).astype(jnp.bfloat16).reshape(
                depth, 1, CORES, utts, HD)
            rest = jnp.where(sel, m + jnp.log(total), 0.0)
            for j in range(PARTS):
                part = rest.astype(jnp.bfloat16).astype(jnp.float32)
                stats = jnp.where(lane == PARTS * h + j, part, stats)
                rest = rest - part
        if k == chunks - 1:
            ctx[k][:, pl.ds(yy, 1), :, :, sizes[k] * HD:] = stats.astype(jnp.bfloat16).reshape(
                depth, 1, CORES, utts, HD)
        return stats

    across = at(z, y_other, c)
    y_in = [[] for _ in range(chunks)]

    def turn(k):
        for dz in (*range(1, depth), 0):
            zz = lax.rem(z + dz, depth)
            cp = remote(ctx[k].at[zz, y_other], ybuf[k].at[dz], y_send.at[k, dz], y_recv.at[k, dz],
                        across)
            cp.start()
            sends.append(cp)
            y_in[k].append((dz, zz, cp))

    stays = []

    def deliver(k):
        slot = 0
        for dz, zz, cp in y_in[k]:
            cp.wait_recv()
            sbuf[k][dz] = ctx[k][pl.ds(zz, 1), pl.ds(y, 1)].reshape(sbuf[k].shape[1:]) + ybuf[k][dz]
            for dc in range(CORES):
                cc = lax.rem(c + dc, CORES)
                if dz == 0 and dc == 0:
                    stay = pltpu.make_async_copy(sbuf[k].at[dz, cc], zbuf[k].at[z, c], stay_sem.at[k])
                    stay.start()
                    stays.append(stay)
                    continue
                cp = remote(sbuf[k].at[dz, cc], zbuf[k].at[z, c], z_send.at[k, slot],
                            z_recv.at[k, z * CORES + c], at(zz, y, cc))
                cp.start()
                sends.append(cp)
                slot += 1

    mask_here, mask_there = masks(y), masks(y_other)
    stats_here = stats_there = jnp.zeros((count, HD), jnp.float32)
    for k in range(chunks):
        piece = qbuf[k].at[z, y, c_other]
        remote(piece, piece, f_send.at[k, 0], q_recv.at[k, partner], partner).wait_recv()
        copies[6 + k].wait()
        if k + 1 < chunks:
            forward(k + 1)
        stats_here = partial(y, mask_here, stats_here, k)
        for zz in range(depth):
            for cc in range(CORES):
                src = at(zz, y_other, cc)
                piece = qbuf[k].at[zz, y_other, cc]
                remote(piece, piece, f_send.at[k, 0], q_recv.at[k, src], src).wait_recv()
        stats_there = partial(y_other, mask_there, stats_there, k)
        turn(k)
        if k == 0:
            for i in range(1, n):
                dev = lax.rem(me + i, n)
                cp = remote(xsend.at[dev], xrecv.at[me], x_send.at[i - 1], x_recv.at[me], dev)
                cp.start()
                sends.append(cp)
        if k > 0:
            deliver(k - 1)

    own = []
    for h in range(feature // HD):
        q = newbuf[:, h * HD : (h + 1) * HD].astype(jnp.float32)
        k = newbuf[:, feature + h * HD : feature + (h + 1) * HD].astype(jnp.float32)
        own.append(jnp.sum(q * k, axis=1, keepdims=True) * scale)

    deliver(chunks - 1)

    own_x.wait()
    for k in range(1, n):
        src = lax.rem(me + n - k, n)
        remote(xsend.at[src], xrecv.at[src], x_send.at[0], x_recv.at[src], src).wait_recv()

    for stay in stays:
        stay.wait()
    for k in range(chunks):
        for dz in range(depth):
            zz = lax.rem(z + dz, depth)
            for dc in range(CORES):
                if dz == 0 and dc == 0:
                    continue
                cc = lax.rem(c + dc, CORES)
                remote(zbuf[k].at[zz, cc], zbuf[k].at[zz, cc], z_send.at[k, 0],
                       z_recv.at[k, zz * CORES + cc], at(zz, y, cc)).wait_recv()

    for cc in range(CORES):
        both = []
        for k in range(chunks):
            both.append(zbuf[k][0, cc].astype(jnp.float32))
            for zz in range(1, depth):
                both[k] = both[k] + zbuf[k][zz, cc].astype(jnp.float32)
        both = jnp.concatenate(both, axis=1)
        stats = both[:, half:]
        lane = lax.broadcasted_iota(jnp.int32, stats.shape, 1)
        for hl in range(heads):
            h = cc * heads + hl
            cols = slice(h * HD, (h + 1) * HD)
            mine = (lane >= PARTS * hl) & (lane < PARTS * (hl + 1))
            lse = jnp.sum(jnp.where(mine, stats, 0.0), axis=1, keepdims=True)
            peak = jnp.maximum(lse, own[h])
            w_old = jnp.exp(lse - peak)
            w_own = jnp.exp(own[h] - peak)
            inv = 1.0 / (w_old + w_own)
            value = newbuf[:, 2 * feature + h * HD : 2 * feature + (h + 1) * HD].astype(jnp.float32)
            self_ctx = both[:, hl * HD : (hl + 1) * HD] * (w_old * inv) + value * (w_own * inv)
            crossed = jnp.concatenate([xrecv[u, :, cols] for u in range(utts)], axis=0)
            out_ref[:, cols] = (
                self_ctx.astype(jnp.bfloat16).astype(jnp.float32) + crossed
            ).astype(jnp.bfloat16)

    for cp in sends:
        cp.wait_send()


def fast_body(n, cache_kv, new_rows, cross_queries, enc_kv, lengths, parents):
    rows, feature = cross_queries.shape
    utts, history, width = cache_kv.shape
    half = feature // CORES
    old = utts * history
    depth = n // (CORES * LINES)
    heads = half // HD
    sizes = chunk_sizes(heads)
    chunks = len(sizes)
    wide = [v * HD for v in sizes[:-1]] + [(sizes[-1] + 1) * HD]
    frames = enc_kv.shape[1]
    bf = jnp.bfloat16
    dma = pltpu.SemaphoreType.DMA
    hbm = pl.BlockSpec(memory_space=pl.ANY)
    return pl.pallas_call(
        functools.partial(fast_kernel, n),
        out_shape=pltpu.VMEM((utts, feature), bf),
        in_specs=[hbm, hbm, hbm, hbm, hbm, hbm],
        out_specs=pl.BlockSpec(memory_space=pltpu.VMEM),
        scratch_shapes=[
            [pltpu.VMEM((depth, LINES, CORES, utts, v * HD), bf) for v in sizes],
            pltpu.VMEM((CORES * old, half), bf),
            pltpu.VMEM((CORES * old, half), bf),
            pltpu.VMEM(new_rows.shape, bf),
            pltpu.VMEM(cross_queries.shape, bf),
            pltpu.VMEM((frames, width), bf),
            pltpu.VMEM((n,) + parents.shape, jnp.int32),
            [pltpu.VMEM((depth, LINES, CORES, utts, v), bf) for v in wide],
            [pltpu.VMEM((depth, CORES, utts, v), bf) for v in wide],
            [pltpu.VMEM((depth, CORES, utts, v), bf) for v in wide],
            [pltpu.VMEM((depth, CORES, utts, v), bf) for v in wide],
            pltpu.VMEM((rows, 1, feature), jnp.float32),
            pltpu.VMEM((utts, 1, feature), jnp.float32),
            dma((8,)),
            dma((chunks, depth * CORES + 1)), dma((chunks, n)), dma((chunks, (depth - 1) * CORES)),
            dma((2,)), dma((2,)),
            dma((n - 1,)), dma((n,)), dma((n - 1,)), dma((n,)),
            dma((chunks, depth)), dma((chunks, depth)),
            dma((chunks, depth * CORES - 1)), dma((chunks, depth * CORES)), dma((chunks,)), dma((chunks,)),
            pltpu.SMEM(lengths.shape, jnp.int32),
        ],
        compiler_params=pltpu.CompilerParams(
            collective_id=0, has_side_effects=True, vmem_limit_bytes=64 * 2**20 - 144 * 1024
        ),
    )(cache_kv.reshape(old, width), new_rows, cross_queries, enc_kv, lengths, parents)


def reorder(cache_rows, parents):
    utterances, beam_width = parents.shape
    grouped = cache_rows.reshape(utterances, beam_width, cache_rows.shape[1], cache_rows.shape[2])
    beams = lax.broadcasted_iota(jnp.int32, (1, 1, beam_width), 2)
    pick = (parents[:, :, None] == beams).astype(cache_rows.dtype)
    picked = jnp.einsum("ubp,uptc->ubtc", pick, grouped, preferred_element_type=jnp.float32)
    return picked.astype(cache_rows.dtype).reshape(cache_rows.shape)


def attend_self(query, old_keys, old_values, new_key, new_value):
    row_count = query.shape[0]
    history = old_keys.shape[1]
    head_count = query.shape[1] // HD
    scale = HD ** (-0.5)
    query_heads = query.reshape(row_count, head_count, HD)
    key_heads = old_keys.reshape(row_count, history, head_count, HD)
    value_heads = old_values.reshape(row_count, history, head_count, HD)
    old_scores = (
        jnp.einsum("rhd,rthd->rht", query_heads, key_heads, preferred_element_type=jnp.float32)
        * scale
    )
    own_score = (
        jnp.einsum(
            "rhd,rhd->rh",
            query_heads,
            new_key.reshape(row_count, head_count, HD),
            preferred_element_type=jnp.float32,
        )
        * scale
    )
    peak = jnp.maximum(jnp.max(old_scores, axis=2), own_score)
    old_exp = jnp.exp(old_scores - peak[:, :, None])
    own_exp = jnp.exp(own_score - peak)
    total = jnp.sum(old_exp, axis=2) + own_exp
    old_weight = (old_exp / total[:, :, None]).astype(jnp.bfloat16)
    own_weight = (own_exp / total).astype(jnp.bfloat16)
    context = jnp.einsum(
        "rht,rthd->rhd", old_weight, value_heads, preferred_element_type=jnp.float32
    )
    context = context + own_weight.astype(jnp.float32)[:, :, None] * new_value.reshape(
        row_count, head_count, HD
    ).astype(jnp.float32)
    return context.reshape(row_count, head_count * HD).astype(jnp.bfloat16)


def attend_frames(queries, frames_kv, frame_counts):
    utterances = frame_counts.shape[0]
    beam_width = queries.shape[0] // utterances
    feature = queries.shape[1]
    head_count = feature // HD
    frame_total = frames_kv.shape[1]
    scale = HD ** (-0.5)
    query_heads = queries.reshape(utterances, beam_width, head_count, HD)
    key_heads = frames_kv[:, :, :feature].reshape(utterances, frame_total, head_count, HD)
    value_heads = frames_kv[:, :, feature:].reshape(utterances, frame_total, head_count, HD)
    scores = (
        jnp.einsum("ubhd,ufhd->uhbf", query_heads, key_heads, preferred_element_type=jnp.float32)
        * scale
    )
    live = (
        lax.broadcasted_iota(jnp.int32, (utterances, 1, 1, frame_total), 3)
        < frame_counts[:, None, None, None]
    )
    scores = jnp.where(live, scores, -1e30)
    peak = jnp.max(scores, axis=3, keepdims=True)
    raised = jnp.where(live, jnp.exp(scores - peak), 0.0)
    weights = (raised / jnp.sum(raised, axis=3, keepdims=True)).astype(jnp.bfloat16)
    context = jnp.einsum(
        "uhbf,ufhd->ubhd", weights, value_heads, preferred_element_type=jnp.float32
    )
    return context.reshape(utterances * beam_width, feature)


def body(cache_kv, new_rows, cross_queries, enc_kv, lengths, parents):
    feature = cross_queries.shape[1]
    cross_context = attend_frames(cross_queries, enc_kv, lengths)
    arrived, new_here = (
        lax.all_to_all(cache_kv, "utt", split_axis=0, concat_axis=0, tiled=True),
        lax.all_to_all(new_rows, "utt", split_axis=0, concat_axis=0, tiled=True),
    )
    reordered = reorder(arrived, parents)
    self_context = attend_self(
        new_here[:, :feature],
        reordered[:, :, :feature],
        reordered[:, :, feature:],
        new_here[:, feature : 2 * feature],
        new_here[:, 2 * feature :],
    )
    mixed_here = (self_context.astype(jnp.float32) + cross_context).astype(jnp.bfloat16)
    mixed = lax.all_to_all(mixed_here, "utt", split_axis=0, concat_axis=0, tiled=True)
    return mixed


def solution(mesh):
    placed = (
        P(("groups", "utt"), None, None),
        P(("groups", "utt"), None),
        P(("groups", "utt"), None),
        P(("groups", "utt"), None, None),
        P(("groups", "utt")),
        P(("groups", "utt"), None),
    )
    n = mesh.shape["utt"]

    def either(cache_kv, new_rows, cross_queries, enc_kv, lengths, parents):
        feature = cross_queries.shape[1]
        fits = (
            parents.shape == (1, n)
            and cache_kv.shape[0] == n
            and n % (CORES * LINES) == 0
            and feature % (CORES * HD) == 0
            and PARTS * (feature // (CORES * HD)) <= HD
        )
        run = functools.partial(fast_body, n) if fits else body
        return run(cache_kv, new_rows, cross_queries, enc_kv, lengths, parents)

    return jax.shard_map(
        either, mesh=mesh, in_specs=placed, out_specs=P(("groups", "utt"), None), check_vma=False
    )
```

```python
import functools

import jax
import jax.numpy as jnp
from jax import lax
from jax.experimental import pallas as pl
from jax.experimental.pallas import tpu as pltpu
from jax.sharding import PartitionSpec as P

HD = 128
TEAM = 4
LOW = -1e30


def contract_last(a, b):
    return lax.dot_general(a, b, (((1,), (1,)), ((), ())), preferred_element_type=jnp.float32)


def fast_kernel(
    n,
    cache_ref, new_ref, cq_ref, enc_ref, len_ref, par_ref,
    out_ref,
    qbuf, kbuf, vbuf, newbuf, cqbuf, encbuf, ptab, xsend, xrecv, cross_ctx,
    ctx, zrecv, fin, fbuf, gbuf, sstat, gstat, len_smem,
    local_sem, own_sem, p_send, p_recv, q_send, q_recv, c_send, c_recv,
    x_send, x_recv, z_send, z_recv, s_send, s_recv, f_send, f_recv, g_send, g_recv,
):
    feature = cq_ref.shape[1]
    quarter = feature // TEAM
    heads = quarter // HD
    rows = cq_ref.shape[0]
    utts = new_ref.shape[0]
    old = cache_ref.shape[0]
    history = old // utts
    depth = n // TEAM
    count = n * utts
    scale = HD ** (-0.5)

    me = lax.axis_index("utt")
    z = me // TEAM
    r = me % TEAM
    others = [k + (k + depth - z) // depth for k in range(depth - 1)]

    def remote(src, dst, ssem, rsem, dev):
        return pltpu.make_async_remote_copy(
            src_ref=src, dst_ref=dst, send_sem=ssem, recv_sem=rsem,
            device_id={"utt": dev}, device_id_type=pl.DeviceIdType.MESH,
        )

    barrier = pltpu.get_barrier_semaphore()
    for k in range(1, n):
        pl.semaphore_signal(
            barrier, inc=1, device_id={"utt": lax.rem(me + k, n)},
            device_id_type=pl.DeviceIdType.MESH,
        )

    def cols(start, size):
        return pl.ds(pl.multiple_of(start, HD), size)

    get_len = pltpu.make_async_copy(len_ref, len_smem, local_sem.at[0])
    get_cq = pltpu.make_async_copy(cq_ref, cqbuf, local_sem.at[1])
    get_enc = pltpu.make_async_copy(enc_ref.at[0], encbuf, local_sem.at[2])
    get_new = pltpu.make_async_copy(new_ref, newbuf, local_sem.at[3])
    get_par = pltpu.make_async_copy(par_ref, ptab.at[me], local_sem.at[4])
    get_q = pltpu.make_async_copy(new_ref.at[:, cols(r * quarter, quarter)], qbuf.at[me], local_sem.at[5])
    for cp in (get_len, get_cq, get_enc, get_q, get_par, get_new):
        cp.start()
    get_own = []
    for h in range(heads):
        pair = []
        for i, buf in enumerate((kbuf, vbuf)):
            cp = pltpu.make_async_copy(
                cache_ref.at[:, cols(i * feature + r * quarter + h * HD, HD)], buf.at[h, r],
                own_sem.at[2 * h + i])
            cp.start()
            pair.append(cp)
        get_own.append(pair)

    frames = encbuf.shape[0]
    ones_f = jnp.ones((frames, HD), jnp.bfloat16)

    def cross(h, live):
        hc = slice(h * HD, (h + 1) * HD)
        s = contract_last(cqbuf[:, hc], encbuf[:, hc]) * scale
        s = jnp.where(live, s, LOW)
        p = jnp.where(live, jnp.exp(s - jnp.max(s, axis=1, keepdims=True)), 0.0).astype(jnp.bfloat16)
        v = jnp.concatenate([encbuf[:, feature + h * HD : feature + (h + 1) * HD], ones_f], axis=1)
        o = jnp.dot(p, v, preferred_element_type=jnp.float32)
        o = o[:, :HD] / o[:, HD:]
        for b in range(rows):
            xsend[b, :, hc] = o[b : b + 1, :]

    pl.semaphore_wait(barrier, n - 1)

    sends = []

    def send(cp):
        cp.start()
        sends.append(cp)
        return cp

    partner = r // 2 * 2 + (1 - r % 2)
    order = [lax.rem(r + 2, TEAM), (1 - r // 2) * 2 + (1 - r % 2), partner]
    for i, rr in enumerate(order):
        send(remote(new_ref.at[:, cols(rr * quarter, quarter)], qbuf.at[me],
                    q_send.at[i], q_recv.at[me], z * TEAM + rr))
    for k, zz in enumerate(others):
        send(remote(new_ref.at[:, cols(r * quarter, quarter)], qbuf.at[me],
                    q_send.at[TEAM - 1 + k], q_recv.at[me], zz * TEAM + r))

    def give(h, i, js):
        buf = (kbuf, vbuf)[i]
        return [send(remote(cache_ref.at[:, cols(i * feature + order[j] * quarter + h * HD, HD)],
                            buf.at[h, r], c_send.at[2 * h + i, j], c_recv.at[2 * h + i, r],
                            z * TEAM + order[j])) for j in js]

    last = heads - 1
    far = tuple(range(TEAM - 2))
    first = [give(h, i, far) for h in range(last) for i in range(2)]
    for k in range(1, n):
        send(remote(par_ref, ptab.at[me], p_send.at[k - 1], p_recv.at[me], lax.rem(me + k, n)))
    for h in range(heads):
        for i in range(2):
            give(h, i, (TEAM - 2,))

    get_len.wait()
    get_cq.wait()
    get_enc.wait()
    live = lax.broadcasted_iota(jnp.int32, (rows, frames), 1) < len_smem[0]
    count_h = feature // HD

    def pass_on(i):
        src = z * TEAM + order[i]
        piece = qbuf.at[src]
        remote(piece, piece, q_send.at[0], q_recv.at[src], src).wait_recv()
        for k, zz in enumerate(others):
            send(remote(piece, piece, q_send.at[TEAM - 1 + (depth - 1) * (i + 1) + k], q_recv.at[src],
                        zz * TEAM + r))

    for h in range(count_h // 4):
        cross(h, live)
    pass_on(TEAM - 2)
    for h in range(count_h // 4, count_h // 2):
        cross(h, live)
    for i in far:
        pass_on(i)
    for h in range(count_h // 2, count_h):
        cross(h, live)
    own_x = pltpu.make_async_copy(xsend.at[me], xrecv.at[me], local_sem.at[6])
    own_x.start()

    def send_x(devs, at):
        for k, dev in enumerate(devs):
            send(remote(xsend.at[dev], xrecv.at[me], x_send.at[at + k], x_recv.at[me], dev))

    side = r // 2 * 2
    near_x = [zz * TEAM + side + c for zz in others for c in range(2)] + [z * TEAM + partner]
    far_x = [zz * TEAM + TEAM - 2 - side + c for zz in (*others, z) for c in range(2)]
    send_x(near_x, 0)

    get_par.wait()
    for k in range(1, n):
        src = lax.rem(me + n - k, n)
        remote(par_ref, ptab.at[src], p_send.at[0], p_recv.at[src], src).wait_recv()
    table = jnp.concatenate([ptab[u] for u in range(utts)], axis=0)
    beam_lane = lax.broadcasted_iota(jnp.int32, table.shape, 1)
    slot = jnp.concatenate(
        [jnp.sum(jnp.where(beam_lane == b, table, 0), axis=1, keepdims=True) for b in range(n)], axis=0)
    slot = jnp.broadcast_to(slot - z * TEAM, (count, old))
    lane = lax.broadcasted_iota(jnp.int32, (count, old), 1)
    row_u = lax.rem(lax.broadcasted_iota(jnp.int32, (count, old), 0), utts)
    own_key = lane // history == row_u
    here = (slot[:, :1] >= 0) & (slot[:, :1] < TEAM)
    spot = lane - row_u

    get_new.wait()
    own = []
    for h in range(feature // HD):
        q = newbuf[:, h * HD : (h + 1) * HD].astype(jnp.float32)
        k = newbuf[:, feature + h * HD : feature + (h + 1) * HD].astype(jnp.float32)
        own.append(jnp.sum(q * k, axis=1, keepdims=True) * scale)

    hold = []
    for i, pair in enumerate(first):
        for cp in pair:
            cp.wait_send()
            hold.append(cp)
        if i == 0:
            give(last, 0, far)
    if not first:
        give(last, 0, far)
    give(last, 1, far)

    get_q.wait()
    for zz in others:
        for t in range(TEAM):
            src = zz * TEAM + t
            piece = qbuf.at[src]
            remote(piece, piece, q_send.at[0], q_recv.at[src], src).wait_recv()

    def arrive(h, i):
        get_own[h][i].wait()
        buf = (kbuf, vbuf)[i]
        for rr in order:
            remote(buf.at[h, rr], buf.at[h, rr], c_send.at[2 * h + i, 0], c_recv.at[2 * h + i, rr],
                   z * TEAM + rr).wait_recv()

    def deliver(h):
        total = ctx[h, pl.ds(z, 1)].reshape(TEAM, utts, HD)
        for zz in others:
            remote(zrecv.at[h, zz], zrecv.at[h, zz], z_send.at[h, 0], z_recv.at[h, zz],
                   zz * TEAM + r).wait_recv()
            total = total + zrecv[h, pl.ds(zz, 1)].reshape(TEAM, utts, HD)
        fin[h] = total
        for i, rr in enumerate(order):
            send(remote(fin.at[h, rr], fbuf.at[r, h], f_send.at[h, i], f_recv.at[r, h], z * TEAM + rr))
        fbuf[pl.ds(r, 1), h] = fin[h, pl.ds(r, 1)]

    team = [(zz, rr) for zz in others for rr in (r, partner, order[0], order[1])]
    team += [(z, rr) for rr in order]
    stats = jnp.zeros((count, HD), jnp.float32)
    for h in range(heads):
        arrive(h, 0)
        q = qbuf[:, :, h * HD : (h + 1) * HD].reshape(count, HD)
        s = contract_last(q, kbuf[h].reshape(TEAM * old, HD))
        picked = s[:, :old]
        for t in range(1, TEAM):
            picked = jnp.where(slot == t, s[:, t * old : (t + 1) * old], picked)
        picked = jnp.where(own_key, picked * scale, LOW)
        m = jnp.max(picked, axis=1, keepdims=True)
        e = jnp.where(own_key, jnp.exp(picked - m), 0.0)
        total = jnp.sum(e, axis=1, keepdims=True)
        e = e * (1.0 / total)
        p = jnp.concatenate(
            [jnp.where(slot == t, e, 0.0).astype(jnp.bfloat16) for t in range(TEAM)], axis=1)
        stats = jnp.where(spot == h * utts, jnp.where(here, m + jnp.log(total), 0.0), stats)
        if h == last:
            for g in range(n):
                sstat[g] = jnp.sum(stats[g * utts : (g + 1) * utts], axis=0, keepdims=True)
            for k, (zz, rr) in enumerate(team):
                send(remote(sstat.at[zz * TEAM + rr], gstat.at[me], s_send.at[k], s_recv.at[me],
                            zz * TEAM + rr))
        arrive(h, 1)
        o = jnp.dot(p, vbuf[h].reshape(TEAM * old, HD), preferred_element_type=jnp.float32)
        ctx[h] = o.astype(jnp.bfloat16).reshape(depth, TEAM, utts, HD)
        if h == last:
            for k, (zz, rr) in enumerate(team):
                send(remote(ctx.at[h, zz, rr], gbuf.at[me], g_send.at[k], g_recv.at[me], zz * TEAM + rr))
        else:
            for k, zz in enumerate(others):
                send(remote(ctx.at[h, zz], zrecv.at[h, z], z_send.at[h, k], z_recv.at[h, z], zz * TEAM + r))
        if h == max(last - 1, 0):
            send_x(far_x, len(near_x))

    for h in range(last):
        deliver(h)
    gbuf[pl.ds(me, 1)] = ctx[last, pl.ds(z, 1), pl.ds(r, 1)].reshape(1, utts, HD)
    gstat[pl.ds(me, 1)] = sstat[pl.ds(me, 1)]

    own_x.wait()
    for k in range(1, n):
        src = lax.rem(me + n - k, n)
        remote(xsend.at[src], xrecv.at[src], x_send.at[0], x_recv.at[src], src).wait_recv()
    for h in range(feature // HD):
        hc = slice(h * HD, (h + 1) * HD)
        cross_ctx[:, hc] = jnp.concatenate([xrecv[u, :, hc] for u in range(utts)], axis=0)

    for k in range(1, n):
        src = lax.rem(me + n - k, n)
        remote(gstat.at[src], gstat.at[src], s_send.at[0], s_recv.at[src], src).wait_recv()
    weights = []
    f_lane = lax.broadcasted_iota(jnp.int32, (utts, HD), 1)
    f_row = lax.broadcasted_iota(jnp.int32, (utts, HD), 0)
    for t in range(TEAM):
        packed = gstat[t]
        for zz in range(1, depth):
            packed = packed + gstat[zz * TEAM + t]
        packed = jnp.broadcast_to(packed, (utts, HD))
        for hl in range(heads):
            lse = jnp.sum(jnp.where(f_lane == f_row + hl * utts, packed, 0.0), axis=1, keepdims=True)
            mine = own[t * heads + hl]
            peak = jnp.maximum(lse, mine)
            w_old = jnp.exp(lse - peak)
            w_own = jnp.exp(mine - peak)
            inv = 1.0 / (w_old + w_own)
            weights.append((w_old * inv, w_own * inv))

    def write(t, hl, got):
        h = t * heads + hl
        hc = slice(h * HD, (h + 1) * HD)
        w_old, w_own = weights[h]
        value = newbuf[:, 2 * feature + h * HD : 2 * feature + (h + 1) * HD].astype(jnp.float32)
        self_ctx = got.astype(jnp.float32) * w_old + value * w_own
        out_ref[:, hc] = (
            self_ctx.astype(jnp.bfloat16).astype(jnp.float32) + cross_ctx[:, hc]
        ).astype(jnp.bfloat16)

    for h in range(last):
        for rr in order:
            remote(fbuf.at[rr, h], fbuf.at[rr, h], f_send.at[h, 0], f_recv.at[rr, h],
                   z * TEAM + rr).wait_recv()
        for t in range(TEAM):
            write(t, h, fbuf[t, h])
    for k in range(1, n):
        src = lax.rem(me + n - k, n)
        remote(gbuf.at[src], gbuf.at[src], g_send.at[0], g_recv.at[src], src).wait_recv()
    for t in range(TEAM):
        got = gbuf[t]
        for zz in range(1, depth):
            got = got + gbuf[zz * TEAM + t]
        write(t, last, got)

    for cp in sends:
        if not any(cp is held for held in hold):
            cp.wait_send()


def fast_body(n, cache_kv, new_rows, cross_queries, enc_kv, lengths, parents):
    rows, feature = cross_queries.shape
    utts, history, width = cache_kv.shape
    old = utts * history
    depth = n // TEAM
    quarter = feature // TEAM
    heads = quarter // HD
    frames = enc_kv.shape[1]
    bf, f32 = jnp.bfloat16, jnp.float32
    dma = pltpu.SemaphoreType.DMA
    hbm = pl.BlockSpec(memory_space=pl.ANY)
    return pl.pallas_call(
        functools.partial(fast_kernel, n),
        out_shape=pltpu.VMEM((utts, feature), bf),
        in_specs=[hbm] * 6,
        out_specs=pl.BlockSpec(memory_space=pltpu.VMEM),
        scratch_shapes=[
            pltpu.VMEM((n, utts, quarter), bf),
            pltpu.VMEM((heads, TEAM, old, HD), bf),
            pltpu.VMEM((heads, TEAM, old, HD), bf),
            pltpu.VMEM(new_rows.shape, bf),
            pltpu.VMEM(cross_queries.shape, bf),
            pltpu.VMEM((frames, width), bf),
            pltpu.VMEM((n,) + parents.shape, jnp.int32),
            pltpu.VMEM((rows, 1, feature), f32),
            pltpu.VMEM((utts, 1, feature), f32),
            pltpu.VMEM((utts, feature), f32),
            pltpu.VMEM((heads, depth, TEAM, utts, HD), bf),
            pltpu.VMEM((heads, depth, TEAM, utts, HD), bf),
            pltpu.VMEM((heads, TEAM, utts, HD), bf),
            pltpu.VMEM((TEAM, heads, utts, HD), bf),
            pltpu.VMEM((n, utts, HD), bf),
            pltpu.VMEM((n, 1, HD), f32),
            pltpu.VMEM((n, 1, HD), f32),
            pltpu.SMEM(lengths.shape, jnp.int32),
            dma((7,)), dma((2 * heads,)), dma((n - 1,)), dma((n,)),
            dma((TEAM - 1 + TEAM * (depth - 1),)), dma((n,)),
            dma((2 * heads, TEAM - 1)), dma((2 * heads, TEAM)),
            dma((n - 1,)), dma((n,)),
            dma((heads, depth - 1)), dma((heads, depth)), dma((n - 1,)), dma((n,)),
            dma((heads, TEAM - 1)), dma((TEAM, heads)), dma((n - 1,)), dma((n,)),
        ],
        compiler_params=pltpu.CompilerParams(
            collective_id=0, has_side_effects=True, vmem_limit_bytes=64 * 2**20 - 144 * 1024
        ),
    )(cache_kv.reshape(old, width), new_rows, cross_queries, enc_kv, lengths, parents)


def reorder(cache_rows, parents):
    utterances, beam_width = parents.shape
    grouped = cache_rows.reshape(utterances, beam_width, cache_rows.shape[1], cache_rows.shape[2])
    beams = lax.broadcasted_iota(jnp.int32, (1, 1, beam_width), 2)
    pick = (parents[:, :, None] == beams).astype(cache_rows.dtype)
    picked = jnp.einsum("ubp,uptc->ubtc", pick, grouped, preferred_element_type=jnp.float32)
    return picked.astype(cache_rows.dtype).reshape(cache_rows.shape)


def attend_self(query, old_keys, old_values, new_key, new_value):
    row_count = query.shape[0]
    history = old_keys.shape[1]
    head_count = query.shape[1] // HD
    scale = HD ** (-0.5)
    query_heads = query.reshape(row_count, head_count, HD)
    key_heads = old_keys.reshape(row_count, history, head_count, HD)
    value_heads = old_values.reshape(row_count, history, head_count, HD)
    old_scores = (
        jnp.einsum("rhd,rthd->rht", query_heads, key_heads, preferred_element_type=jnp.float32)
        * scale
    )
    own_score = (
        jnp.einsum(
            "rhd,rhd->rh",
            query_heads,
            new_key.reshape(row_count, head_count, HD),
            preferred_element_type=jnp.float32,
        )
        * scale
    )
    peak = jnp.maximum(jnp.max(old_scores, axis=2), own_score)
    old_exp = jnp.exp(old_scores - peak[:, :, None])
    own_exp = jnp.exp(own_score - peak)
    total = jnp.sum(old_exp, axis=2) + own_exp
    old_weight = (old_exp / total[:, :, None]).astype(jnp.bfloat16)
    own_weight = (own_exp / total).astype(jnp.bfloat16)
    context = jnp.einsum(
        "rht,rthd->rhd", old_weight, value_heads, preferred_element_type=jnp.float32
    )
    context = context + own_weight.astype(jnp.float32)[:, :, None] * new_value.reshape(
        row_count, head_count, HD
    ).astype(jnp.float32)
    return context.reshape(row_count, head_count * HD).astype(jnp.bfloat16)


def attend_frames(queries, frames_kv, frame_counts):
    utterances = frame_counts.shape[0]
    beam_width = queries.shape[0] // utterances
    feature = queries.shape[1]
    head_count = feature // HD
    frame_total = frames_kv.shape[1]
    scale = HD ** (-0.5)
    query_heads = queries.reshape(utterances, beam_width, head_count, HD)
    key_heads = frames_kv[:, :, :feature].reshape(utterances, frame_total, head_count, HD)
    value_heads = frames_kv[:, :, feature:].reshape(utterances, frame_total, head_count, HD)
    scores = (
        jnp.einsum("ubhd,ufhd->uhbf", query_heads, key_heads, preferred_element_type=jnp.float32)
        * scale
    )
    live = (
        lax.broadcasted_iota(jnp.int32, (utterances, 1, 1, frame_total), 3)
        < frame_counts[:, None, None, None]
    )
    scores = jnp.where(live, scores, -1e30)
    peak = jnp.max(scores, axis=3, keepdims=True)
    raised = jnp.where(live, jnp.exp(scores - peak), 0.0)
    weights = (raised / jnp.sum(raised, axis=3, keepdims=True)).astype(jnp.bfloat16)
    context = jnp.einsum(
        "uhbf,ufhd->ubhd", weights, value_heads, preferred_element_type=jnp.float32
    )
    return context.reshape(utterances * beam_width, feature)


def body(cache_kv, new_rows, cross_queries, enc_kv, lengths, parents):
    feature = cross_queries.shape[1]
    cross_context = attend_frames(cross_queries, enc_kv, lengths)
    arrived, new_here = (
        lax.all_to_all(cache_kv, "utt", split_axis=0, concat_axis=0, tiled=True),
        lax.all_to_all(new_rows, "utt", split_axis=0, concat_axis=0, tiled=True),
    )
    reordered = reorder(arrived, parents)
    self_context = attend_self(
        new_here[:, :feature],
        reordered[:, :, :feature],
        reordered[:, :, feature:],
        new_here[:, feature : 2 * feature],
        new_here[:, 2 * feature :],
    )
    mixed_here = (self_context.astype(jnp.float32) + cross_context).astype(jnp.bfloat16)
    mixed = lax.all_to_all(mixed_here, "utt", split_axis=0, concat_axis=0, tiled=True)
    return mixed


def solution(mesh):
    placed = (
        P(("groups", "utt"), None, None),
        P(("groups", "utt"), None),
        P(("groups", "utt"), None),
        P(("groups", "utt"), None, None),
        P(("groups", "utt")),
        P(("groups", "utt"), None),
    )
    n = mesh.shape["utt"]

    def either(cache_kv, new_rows, cross_queries, enc_kv, lengths, parents):
        feature = cross_queries.shape[1]
        fits = (
            parents.shape == (1, n)
            and cache_kv.shape[0] == n
            and n % TEAM == 0
            and n > TEAM
            and feature % (TEAM * HD) == 0
            and cache_kv.shape[0] * cache_kv.shape[1] == HD
            and feature // (TEAM * HD) * n <= HD
        )
        run = functools.partial(fast_body, n) if fits else body
        return run(cache_kv, new_rows, cross_queries, enc_kv, lengths, parents)

    return jax.shard_map(
        either, mesh=mesh, in_specs=placed, out_specs=P(("groups", "utt"), None), check_vma=False
    )
```

```python
import functools

import jax
import jax.numpy as jnp
from jax import lax
from jax.experimental import pallas as pl
from jax.experimental.pallas import tpu as pltpu
from jax.sharding import PartitionSpec as P

HD = 128
TEAM = 4
CORES = 2
LOW = -1e30


def contract_last(a, b):
    return lax.dot_general(a, b, (((1,), (1,)), ((), ())), preferred_element_type=jnp.float32)


def fast_kernel(
    n,
    cache_ref, new_ref, cq_ref, enc_ref, len_ref, par_ref,
    out_ref,
    qbuf, kbuf, vbuf, newbuf, cqbuf, encbuf, ptab, xsend, xrecv, cross_ctx,
    ctx, gbuf, sstat, gstat, len_smem,
    local_sem, own_sem, p_send, p_recv, q_send, q_recv, c_send, c_recv,
    x_send, x_recv, s_send, s_recv, g_send, g_recv, ready,
):
    feature = cq_ref.shape[1]
    quarter = feature // TEAM
    heads = quarter // HD
    rows = cq_ref.shape[0]
    utts = new_ref.shape[0]
    old = cache_ref.shape[0]
    history = old // utts
    depth = n // TEAM
    count = n * utts
    scale = HD ** (-0.5)

    me = lax.axis_index("utt")
    z = me // TEAM
    r = me % TEAM
    others = [k + (k + depth - z) // depth for k in range(depth - 1)]

    def remote(src, dst, ssem, rsem, dev):
        return pltpu.make_async_remote_copy(
            src_ref=src, dst_ref=dst, send_sem=ssem, recv_sem=rsem,
            device_id={"utt": dev}, device_id_type=pl.DeviceIdType.MESH,
        )

    core = r % CORES
    partner = r + 1 - 2 * core
    order = [lax.rem(r + CORES, TEAM), lax.rem(partner + CORES, TEAM), partner]

    def tell(sem, dev):
        pl.semaphore_signal(sem, inc=1, device_id={"utt": dev}, device_id_type=pl.DeviceIdType.MESH)

    barrier = pltpu.get_barrier_semaphore()
    tell(barrier, z * TEAM + lax.rem(r - core + CORES, TEAM))

    @pl.when(core == 1)
    def _():
        tell(barrier, z * TEAM + partner)

    for zz in others:
        for t in range(1, TEAM, CORES):
            tell(barrier, zz * TEAM + t)

    def cols(start, size):
        return pl.ds(pl.multiple_of(start, HD), size)

    get_len = pltpu.make_async_copy(len_ref, len_smem, local_sem.at[0])
    get_cq = pltpu.make_async_copy(cq_ref, cqbuf, local_sem.at[1])
    get_enc = pltpu.make_async_copy(enc_ref.at[0], encbuf, local_sem.at[2])
    get_new = pltpu.make_async_copy(new_ref, newbuf, local_sem.at[3])
    get_par = pltpu.make_async_copy(par_ref, ptab.at[me], local_sem.at[4])
    get_q = pltpu.make_async_copy(new_ref.at[:, cols(r * quarter, quarter)], qbuf.at[me], local_sem.at[5])
    for cp in (get_len, get_cq, get_enc, get_q, get_par, get_new):
        cp.start()
    get_own = []
    for h in range(heads):
        pair = []
        for i, buf in enumerate((kbuf, vbuf)):
            cp = pltpu.make_async_copy(
                cache_ref.at[:, cols(i * feature + r * quarter + h * HD, HD)], buf.at[h, r],
                own_sem.at[2 * h + i])
            cp.start()
            pair.append(cp)
        get_own.append(pair)

    frames = encbuf.shape[0]
    ones_f = jnp.ones((frames, HD), jnp.bfloat16)

    crossed = []

    def cross(h, live):
        hc = slice(h * HD, (h + 1) * HD)
        s = contract_last(cqbuf[:, hc], encbuf[:, hc]) * scale
        s = jnp.where(live, s, LOW)
        p = jnp.where(live, jnp.exp(s - jnp.max(s, axis=1, keepdims=True)), 0.0).astype(jnp.bfloat16)
        v = jnp.concatenate([encbuf[:, feature + h * HD : feature + (h + 1) * HD], ones_f], axis=1)
        o = jnp.dot(p, v, preferred_element_type=jnp.float32)
        crossed.append((o[:, :HD] / o[:, HD:]).astype(jnp.bfloat16))

    @pl.when(core == 0)
    def _():
        pl.semaphore_wait(barrier, TEAM - 1)
        tell(ready, z * TEAM + partner)

    @pl.when(core == 1)
    def _():
        pl.semaphore_wait(ready, 1)

    sends = []

    def send(cp):
        cp.start()
        sends.append(cp)
        return cp

    far = tuple(range(TEAM - 2))
    def ask(i):
        send(remote(new_ref.at[:, cols(order[i] * quarter, quarter)], qbuf.at[me],
                    q_send.at[i], q_recv.at[me], z * TEAM + order[i]))
        send(remote(par_ref, ptab.at[me], p_send.at[i], p_recv.at[me], z * TEAM + order[i]))

    for i in range(TEAM - 1):
        ask(i)

    def give(h, i, js):
        buf = (kbuf, vbuf)[i]
        return [send(remote(cache_ref.at[:, cols(i * feature + order[j] * quarter + h * HD, HD)],
                            buf.at[h, r], c_send.at[2 * h + i, j], c_recv.at[2 * h + i, r],
                            z * TEAM + order[j])) for j in js]

    last = heads - 1
    give(0, 0, far)
    give(0, 1, far)
    stream = [(h, i) for i in range(2) for h in range(1, heads)]
    if heads > 2:
        stream = [(1, 0), (2, 0), (1, 1), (2, 1)] + [(h, i) for h in range(3, heads) for i in range(2)]
    for h, i in stream:
        give(h, i, far)
    for h in range(heads):
        for i in range(2):
            give(h, i, (TEAM - 2,))

    get_len.wait()
    get_cq.wait()
    get_enc.wait()
    live = lax.broadcasted_iota(jnp.int32, (rows, frames), 1) < len_smem[0]
    count_h = feature // HD

    def pass_on(i):
        src = z * TEAM + order[i]
        piece = qbuf.at[src]
        remote(piece, piece, q_send.at[0], q_recv.at[src], src).wait_recv()
        remote(par_ref, ptab.at[src], p_send.at[0], p_recv.at[src], src).wait_recv()
        for k, zz in enumerate(others):
            spot = TEAM - 1 + (depth - 1) * (i + 1) + k
            send(remote(piece, piece, q_send.at[spot], q_recv.at[src], zz * TEAM + r))
            send(remote(ptab.at[src], ptab.at[src], p_send.at[spot], p_recv.at[src], zz * TEAM + r))

    for h in range(count_h // 4):
        cross(h, live)

    @pl.when(core == 1)
    def _():
        pl.semaphore_wait(barrier, n - TEAM)
        tell(ready, z * TEAM + partner)

    @pl.when(core == 0)
    def _():
        pl.semaphore_wait(ready, 1)

    for k, zz in enumerate(others):
        send(remote(new_ref.at[:, cols(r * quarter, quarter)], qbuf.at[me],
                    q_send.at[TEAM - 1 + k], q_recv.at[me], zz * TEAM + r))
        send(remote(par_ref, ptab.at[me], p_send.at[TEAM - 1 + k], p_recv.at[me], zz * TEAM + r))
    pass_on(TEAM - 2)
    for h in range(count_h // 4, count_h // 2):
        cross(h, live)
    for i in far:
        pass_on(i)
    for h in range(count_h // 2, count_h):
        cross(h, live)
    pad = xsend.shape[1]
    to_row = lax.broadcasted_iota(jnp.int32, (rows * pad, rows * count_h), 0)
    from_row = lax.broadcasted_iota(jnp.int32, (rows * pad, rows * count_h), 1)
    turn = (to_row // pad == from_row % rows) & (to_row % pad == from_row // rows)
    turned = jnp.dot(turn.astype(jnp.bfloat16), jnp.concatenate(crossed, axis=0),
                     preferred_element_type=jnp.float32)
    xsend[...] = turned.astype(jnp.bfloat16).reshape(xsend.shape)
    own_x = pltpu.make_async_copy(xsend.at[me], xrecv.at[me], local_sem.at[6])
    own_x.start()

    def send_x(devs, at):
        for k, dev in enumerate(devs):
            send(remote(xsend.at[dev], xrecv.at[me], x_send.at[at + k], x_recv.at[me], dev))

    side = r // 2 * 2
    near_x = [zz * TEAM + side + c for zz in others for c in range(2)] + [z * TEAM + partner]
    far_x = [zz * TEAM + TEAM - 2 - side + c for zz in (*others, z) for c in range(2)]
    send_x(near_x, 0)
    send_x(far_x, len(near_x))

    get_par.wait()
    for zz in others:
        for t in range(TEAM):
            src = zz * TEAM + t
            remote(par_ref, ptab.at[src], p_send.at[0], p_recv.at[src], src).wait_recv()
    table = jnp.concatenate([ptab[u] for u in range(utts)], axis=0)
    beam_lane = lax.broadcasted_iota(jnp.int32, table.shape, 1)
    slot = jnp.concatenate(
        [jnp.sum(jnp.where(beam_lane == b, table, 0), axis=1, keepdims=True) for b in range(n)], axis=0)
    slot = jnp.broadcast_to(slot - z * TEAM, (count, old))
    lane = lax.broadcasted_iota(jnp.int32, (count, old), 1)
    row_u = lax.rem(lax.broadcasted_iota(jnp.int32, (count, old), 0), utts)
    own_key = lane // history == row_u
    here = (slot[:, :1] >= 0) & (slot[:, :1] < TEAM)
    spot = lane - row_u

    get_new.wait()
    own = []
    for h in range(feature // HD):
        q = newbuf[:, h * HD : (h + 1) * HD].astype(jnp.float32)
        k = newbuf[:, feature + h * HD : feature + (h + 1) * HD].astype(jnp.float32)
        own.append(jnp.sum(q * k, axis=1, keepdims=True) * scale)

    get_q.wait()
    for zz in others:
        for t in range(TEAM):
            src = zz * TEAM + t
            piece = qbuf.at[src]
            remote(piece, piece, q_send.at[0], q_recv.at[src], src).wait_recv()

    def arrive(h, i):
        get_own[h][i].wait()
        buf = (kbuf, vbuf)[i]
        for rr in order:
            remote(buf.at[h, rr], buf.at[h, rr], c_send.at[2 * h + i, 0], c_recv.at[2 * h + i, rr],
                   z * TEAM + rr).wait_recv()

    team = [(zz, rr) for zz in others for rr in (r, partner, order[0], order[1])]
    team += [(z, rr) for rr in order]
    stats = jnp.zeros((count, HD), jnp.float32)
    weight = []

    def score(h):
        arrive(h, 0)
        q = qbuf[:, :, h * HD : (h + 1) * HD].reshape(count, HD)
        s = contract_last(q, kbuf[h].reshape(TEAM * old, HD))
        picked = s[:, :old]
        for t in range(1, TEAM):
            picked = jnp.where(slot == t, s[:, t * old : (t + 1) * old], picked)
        picked = jnp.where(own_key, picked * scale, LOW)
        m = jnp.max(picked, axis=1, keepdims=True)
        e = jnp.where(own_key, jnp.exp(picked - m), 0.0)
        total = jnp.sum(e, axis=1, keepdims=True)
        e = e * (1.0 / total)
        weight.append(jnp.concatenate(
            [jnp.where(slot == t, e, 0.0).astype(jnp.bfloat16) for t in range(TEAM)], axis=1))
        return jnp.where(spot == h * utts, jnp.where(here, m + jnp.log(total), 0.0), stats)

    def give_back(h):
        arrive(h, 1)
        o = jnp.dot(weight[h], vbuf[h].reshape(TEAM * old, HD), preferred_element_type=jnp.float32)
        ctx[h] = o.astype(jnp.bfloat16).reshape(depth, TEAM, utts, HD)
        for k, (zz, rr) in enumerate(team):
            send(remote(ctx.at[h, zz, rr], gbuf.at[h, me], g_send.at[h, k], g_recv.at[h, me],
                        zz * TEAM + rr))
        gbuf[h, pl.ds(me, 1)] = ctx[h, pl.ds(z, 1), pl.ds(r, 1)].reshape(1, utts, HD)

    stats = score(0)
    give_back(0)
    for h in range(1, heads):
        stats = score(h)
    for g in range(n):
        sstat[g] = jnp.sum(stats[g * utts : (g + 1) * utts], axis=0, keepdims=True)
    for k, (zz, rr) in enumerate(team):
        send(remote(sstat.at[zz * TEAM + rr], gstat.at[me], s_send.at[k], s_recv.at[me], zz * TEAM + rr))
    for h in range(1, heads):
        give_back(h)

    gstat[pl.ds(me, 1)] = sstat[pl.ds(me, 1)]

    own_x.wait()
    for k in range(1, n):
        src = lax.rem(me + n - k, n)
        remote(xsend.at[src], xrecv.at[src], x_send.at[0], x_recv.at[src], src).wait_recv()
    to_row = lax.broadcasted_iota(jnp.int32, (utts * count_h, utts * pad), 0)
    from_row = lax.broadcasted_iota(jnp.int32, (utts * count_h, utts * pad), 1)
    turn = (to_row % utts == from_row // pad) & (to_row // utts == from_row % pad)
    cross_ctx[...] = jnp.dot(turn.astype(jnp.bfloat16), xrecv[...].reshape(utts * pad, HD),
                             preferred_element_type=jnp.float32)

    for k in range(1, n):
        src = lax.rem(me + n - k, n)
        remote(gstat.at[src], gstat.at[src], s_send.at[0], s_recv.at[src], src).wait_recv()
    weights = []
    f_lane = lax.broadcasted_iota(jnp.int32, (utts, HD), 1)
    f_row = lax.broadcasted_iota(jnp.int32, (utts, HD), 0)
    for t in range(TEAM):
        packed = gstat[t]
        for zz in range(1, depth):
            packed = packed + gstat[zz * TEAM + t]
        packed = jnp.broadcast_to(packed, (utts, HD))
        for hl in range(heads):
            lse = jnp.sum(jnp.where(f_lane == f_row + hl * utts, packed, 0.0), axis=1, keepdims=True)
            mine = own[t * heads + hl]
            peak = jnp.maximum(lse, mine)
            w_old = jnp.exp(lse - peak)
            w_own = jnp.exp(mine - peak)
            inv = 1.0 / (w_old + w_own)
            weights.append((w_old * inv, w_own * inv))

    def write(t, hl):
        h = t * heads + hl
        hc = slice(h * HD, (h + 1) * HD)
        got = gbuf[hl, t]
        for zz in range(1, depth):
            got = got + gbuf[hl, zz * TEAM + t]
        w_old, w_own = weights[h]
        value = newbuf[:, 2 * feature + h * HD : 2 * feature + (h + 1) * HD].astype(jnp.float32)
        self_ctx = got.astype(jnp.float32) * w_old + value * w_own
        out_ref[:, hc] = (
            self_ctx.astype(jnp.bfloat16).astype(jnp.float32) + cross_ctx[h * utts : (h + 1) * utts]
        ).astype(jnp.bfloat16)

    for hl in range(heads):
        for k in range(1, n):
            src = lax.rem(me + n - k, n)
            remote(gbuf.at[hl, src], gbuf.at[hl, src], g_send.at[hl, 0], g_recv.at[hl, src], src).wait_recv()
        for t in range(TEAM):
            write(t, hl)

    for cp in sends:
        cp.wait_send()


def fast_body(n, cache_kv, new_rows, cross_queries, enc_kv, lengths, parents):
    rows, feature = cross_queries.shape
    utts, history, width = cache_kv.shape
    old = utts * history
    depth = n // TEAM
    quarter = feature // TEAM
    heads = quarter // HD
    frames = enc_kv.shape[1]
    pad = -(-(feature // HD) // 8) * 8
    bf, f32 = jnp.bfloat16, jnp.float32
    dma = pltpu.SemaphoreType.DMA
    hbm = pl.BlockSpec(memory_space=pl.ANY)
    return pl.pallas_call(
        functools.partial(fast_kernel, n),
        out_shape=pltpu.VMEM((utts, feature), bf),
        in_specs=[hbm] * 6,
        out_specs=pl.BlockSpec(memory_space=pltpu.VMEM),
        scratch_shapes=[
            pltpu.VMEM((n, utts, quarter), bf),
            pltpu.VMEM((heads, TEAM, old, HD), bf),
            pltpu.VMEM((heads, TEAM, old, HD), bf),
            pltpu.VMEM(new_rows.shape, bf),
            pltpu.VMEM(cross_queries.shape, bf),
            pltpu.VMEM((frames, width), bf),
            pltpu.VMEM((n,) + parents.shape, jnp.int32),
            pltpu.VMEM((rows, pad, HD), bf),
            pltpu.VMEM((utts, pad, HD), bf),
            pltpu.VMEM((utts * (feature // HD), HD), f32),
            pltpu.VMEM((heads, depth, TEAM, utts, HD), bf),
            pltpu.VMEM((heads, n, utts, HD), bf),
            pltpu.VMEM((n, 1, HD), f32),
            pltpu.VMEM((n, 1, HD), f32),
            pltpu.SMEM(lengths.shape, jnp.int32),
            dma((7,)), dma((2 * heads,)), dma((TEAM - 1 + TEAM * (depth - 1),)), dma((n,)),
            dma((TEAM - 1 + TEAM * (depth - 1),)), dma((n,)),
            dma((2 * heads, TEAM - 1)), dma((2 * heads, TEAM)),
            dma((n - 1,)), dma((n,)), dma((n - 1,)), dma((n,)),
            dma((heads, n - 1)), dma((heads, n)), pltpu.SemaphoreType.REGULAR,
        ],
        compiler_params=pltpu.CompilerParams(
            collective_id=0, has_side_effects=True, vmem_limit_bytes=64 * 2**20 - 144 * 1024
        ),
    )(cache_kv.reshape(old, width), new_rows, cross_queries, enc_kv, lengths, parents)


def reorder(cache_rows, parents):
    utterances, beam_width = parents.shape
    grouped = cache_rows.reshape(utterances, beam_width, cache_rows.shape[1], cache_rows.shape[2])
    beams = lax.broadcasted_iota(jnp.int32, (1, 1, beam_width), 2)
    pick = (parents[:, :, None] == beams).astype(cache_rows.dtype)
    picked = jnp.einsum("ubp,uptc->ubtc", pick, grouped, preferred_element_type=jnp.float32)
    return picked.astype(cache_rows.dtype).reshape(cache_rows.shape)


def attend_self(query, old_keys, old_values, new_key, new_value):
    row_count = query.shape[0]
    history = old_keys.shape[1]
    head_count = query.shape[1] // HD
    scale = HD ** (-0.5)
    query_heads = query.reshape(row_count, head_count, HD)
    key_heads = old_keys.reshape(row_count, history, head_count, HD)
    value_heads = old_values.reshape(row_count, history, head_count, HD)
    old_scores = (
        jnp.einsum("rhd,rthd->rht", query_heads, key_heads, preferred_element_type=jnp.float32)
        * scale
    )
    own_score = (
        jnp.einsum(
            "rhd,rhd->rh",
            query_heads,
            new_key.reshape(row_count, head_count, HD),
            preferred_element_type=jnp.float32,
        )
        * scale
    )
    peak = jnp.maximum(jnp.max(old_scores, axis=2), own_score)
    old_exp = jnp.exp(old_scores - peak[:, :, None])
    own_exp = jnp.exp(own_score - peak)
    total = jnp.sum(old_exp, axis=2) + own_exp
    old_weight = (old_exp / total[:, :, None]).astype(jnp.bfloat16)
    own_weight = (own_exp / total).astype(jnp.bfloat16)
    context = jnp.einsum(
        "rht,rthd->rhd", old_weight, value_heads, preferred_element_type=jnp.float32
    )
    context = context + own_weight.astype(jnp.float32)[:, :, None] * new_value.reshape(
        row_count, head_count, HD
    ).astype(jnp.float32)
    return context.reshape(row_count, head_count * HD).astype(jnp.bfloat16)


def attend_frames(queries, frames_kv, frame_counts):
    utterances = frame_counts.shape[0]
    beam_width = queries.shape[0] // utterances
    feature = queries.shape[1]
    head_count = feature // HD
    frame_total = frames_kv.shape[1]
    scale = HD ** (-0.5)
    query_heads = queries.reshape(utterances, beam_width, head_count, HD)
    key_heads = frames_kv[:, :, :feature].reshape(utterances, frame_total, head_count, HD)
    value_heads = frames_kv[:, :, feature:].reshape(utterances, frame_total, head_count, HD)
    scores = (
        jnp.einsum("ubhd,ufhd->uhbf", query_heads, key_heads, preferred_element_type=jnp.float32)
        * scale
    )
    live = (
        lax.broadcasted_iota(jnp.int32, (utterances, 1, 1, frame_total), 3)
        < frame_counts[:, None, None, None]
    )
    scores = jnp.where(live, scores, -1e30)
    peak = jnp.max(scores, axis=3, keepdims=True)
    raised = jnp.where(live, jnp.exp(scores - peak), 0.0)
    weights = (raised / jnp.sum(raised, axis=3, keepdims=True)).astype(jnp.bfloat16)
    context = jnp.einsum(
        "uhbf,ufhd->ubhd", weights, value_heads, preferred_element_type=jnp.float32
    )
    return context.reshape(utterances * beam_width, feature)


def body(cache_kv, new_rows, cross_queries, enc_kv, lengths, parents):
    feature = cross_queries.shape[1]
    cross_context = attend_frames(cross_queries, enc_kv, lengths)
    arrived, new_here = (
        lax.all_to_all(cache_kv, "utt", split_axis=0, concat_axis=0, tiled=True),
        lax.all_to_all(new_rows, "utt", split_axis=0, concat_axis=0, tiled=True),
    )
    reordered = reorder(arrived, parents)
    self_context = attend_self(
        new_here[:, :feature],
        reordered[:, :, :feature],
        reordered[:, :, feature:],
        new_here[:, feature : 2 * feature],
        new_here[:, 2 * feature :],
    )
    mixed_here = (self_context.astype(jnp.float32) + cross_context).astype(jnp.bfloat16)
    mixed = lax.all_to_all(mixed_here, "utt", split_axis=0, concat_axis=0, tiled=True)
    return mixed


def solution(mesh):
    placed = (
        P(("groups", "utt"), None, None),
        P(("groups", "utt"), None),
        P(("groups", "utt"), None),
        P(("groups", "utt"), None, None),
        P(("groups", "utt")),
        P(("groups", "utt"), None),
    )
    n = mesh.shape["utt"]

    def either(cache_kv, new_rows, cross_queries, enc_kv, lengths, parents):
        feature = cross_queries.shape[1]
        fits = (
            parents.shape == (1, n)
            and cache_kv.shape[0] == n
            and n % TEAM == 0
            and n > TEAM
            and feature % (TEAM * HD) == 0
            and cache_kv.shape[0] * cache_kv.shape[1] == HD
            and feature // (TEAM * HD) * n <= HD
        )
        run = functools.partial(fast_body, n) if fits else body
        return run(cache_kv, new_rows, cross_queries, enc_kv, lengths, parents)

    return jax.shard_map(
        either, mesh=mesh, in_specs=placed, out_specs=P(("groups", "utt"), None), check_vma=False
    )
```

```python
import functools

import jax
import jax.numpy as jnp
from jax import lax
from jax.experimental import pallas as pl
from jax.experimental.pallas import tpu as pltpu
from jax.sharding import PartitionSpec as P

HD = 128
TEAM = 4
CORES = 2
LOW = -1e30


def contract_last(a, b):
    return lax.dot_general(a, b, (((1,), (1,)), ((), ())), preferred_element_type=jnp.float32)


def fast_kernel(
    n,
    cache_ref, new_ref, cq_ref, enc_ref, len_ref, par_ref,
    out_ref,
    qbuf, kbuf, vbuf, newbuf, cqbuf, encbuf, ptab, xsend, xrecv, cross_ctx,
    ctx, gbuf, sstat, gstat, len_smem,
    local_sem, own_sem, p_send, p_recv, pz_recv, q_send, q_recv, qz_recv, c_send, c_recv,
    x_send, x_recv, s_send, s_recv, g_send, g_recv, ready,
):
    feature = cq_ref.shape[1]
    quarter = feature // TEAM
    heads = quarter // HD
    rows = cq_ref.shape[0]
    utts = new_ref.shape[0]
    old = cache_ref.shape[0]
    history = old // utts
    depth = n // TEAM
    count = n * utts
    scale = HD ** (-0.5)

    me = lax.axis_index("utt")
    z = me // TEAM
    r = me % TEAM
    others = [k + (k + depth - z) // depth for k in range(depth - 1)]
    upper = 2 * z // depth
    downward = [depth - 2 - k + (2 * depth - 2 - k - z) // depth for k in range(depth - 1)]
    far_first = [upper * a + (1 - upper) * b for a, b in zip(others, downward)]

    def remote(src, dst, ssem, rsem, dev):
        return pltpu.make_async_remote_copy(
            src_ref=src, dst_ref=dst, send_sem=ssem, recv_sem=rsem,
            device_id={"utt": dev}, device_id_type=pl.DeviceIdType.MESH,
        )

    core = r % CORES
    partner = r + 1 - 2 * core
    order = [lax.rem(r + CORES, TEAM), lax.rem(partner + CORES, TEAM), partner]

    def tell(sem, dev):
        pl.semaphore_signal(sem, inc=1, device_id={"utt": dev}, device_id_type=pl.DeviceIdType.MESH)

    barrier = pltpu.get_barrier_semaphore()
    tell(barrier, z * TEAM + lax.rem(r - core + CORES, TEAM))

    @pl.when(core == 1)
    def _():
        tell(barrier, z * TEAM + partner)

    for zz in others:
        for t in range(1, TEAM, CORES):
            tell(barrier, zz * TEAM + t)

    def cols(start, size):
        return pl.ds(pl.multiple_of(start, HD), size)

    get_len = pltpu.make_async_copy(len_ref, len_smem, local_sem.at[0])
    get_cq = pltpu.make_async_copy(cq_ref, cqbuf, local_sem.at[1])
    get_enc = pltpu.make_async_copy(enc_ref.at[0], encbuf, local_sem.at[2])
    get_new = pltpu.make_async_copy(new_ref, newbuf, local_sem.at[3])
    get_par = pltpu.make_async_copy(par_ref, ptab.at[me], local_sem.at[4])
    get_q = pltpu.make_async_copy(new_ref.at[:, cols(r * quarter, quarter)], qbuf.at[me], local_sem.at[5])
    for cp in (get_len, get_cq, get_enc, get_q, get_par, get_new):
        cp.start()
    get_own = []
    for h in range(heads):
        pair = []
        for i, buf in enumerate((kbuf, vbuf)):
            cp = pltpu.make_async_copy(
                cache_ref.at[:, cols(i * feature + r * quarter + h * HD, HD)], buf.at[h, r],
                own_sem.at[2 * h + i])
            cp.start()
            pair.append(cp)
        get_own.append(pair)

    frames = encbuf.shape[0]
    ones_f = jnp.ones((frames, HD), jnp.bfloat16)

    crossed = []

    def cross(h, live):
        hc = slice(h * HD, (h + 1) * HD)
        s = contract_last(cqbuf[:, hc], encbuf[:, hc]) * scale
        s = jnp.where(live, s, LOW)
        p = jnp.where(live, jnp.exp(s - jnp.max(s, axis=1, keepdims=True)), 0.0).astype(jnp.bfloat16)
        v = jnp.concatenate([encbuf[:, feature + h * HD : feature + (h + 1) * HD], ones_f], axis=1)
        o = jnp.dot(p, v, preferred_element_type=jnp.float32)
        crossed.append((o[:, :HD] / o[:, HD:]).astype(jnp.bfloat16))

    @pl.when(core == 0)
    def _():
        pl.semaphore_wait(barrier, TEAM - 1)
        tell(ready, z * TEAM + partner)

    @pl.when(core == 1)
    def _():
        pl.semaphore_wait(ready, 1)

    sends = []

    def send(cp):
        cp.start()
        sends.append(cp)
        return cp

    far = tuple(range(TEAM - 2))
    def ask(i):
        send(remote(new_ref.at[:, cols(order[i] * quarter, quarter)], qbuf.at[me],
                    q_send.at[i], q_recv.at[me], z * TEAM + order[i]))
        send(remote(par_ref, ptab.at[me], p_send.at[i], p_recv.at[me], z * TEAM + order[i]))

    for i in range(TEAM - 1):
        ask(i)

    def give(h, i, js):
        buf = (kbuf, vbuf)[i]
        return [send(remote(cache_ref.at[:, cols(i * feature + order[j] * quarter + h * HD, HD)],
                            buf.at[h, r], c_send.at[2 * h + i, j], c_recv.at[2 * h + i, r],
                            z * TEAM + order[j])) for j in js]

    last = heads - 1
    give(0, 0, far)
    give(0, 1, far)
    stream = [(h, i) for i in range(2) for h in range(1, heads)]
    if heads > 2:
        stream = [(1, 0), (2, 0), (1, 1), (2, 1)] + [(h, i) for h in range(3, heads) for i in range(2)]
    for h, i in stream:
        give(h, i, far)
    for h in range(heads):
        for i in range(2):
            give(h, i, (TEAM - 2,))

    get_len.wait()
    get_cq.wait()
    get_enc.wait()
    live = lax.broadcasted_iota(jnp.int32, (rows, frames), 1) < len_smem[0]
    count_h = feature // HD

    for h in range(count_h):
        cross(h, live)
    pad = xsend.shape[1]
    to_row = lax.broadcasted_iota(jnp.int32, (rows * pad, rows * count_h), 0)
    from_row = lax.broadcasted_iota(jnp.int32, (rows * pad, rows * count_h), 1)
    turn = (to_row // pad == from_row % rows) & (to_row % pad == from_row // rows)
    turned = jnp.dot(turn.astype(jnp.bfloat16), jnp.concatenate(crossed, axis=0),
                     preferred_element_type=jnp.float32)
    xsend[...] = turned.astype(jnp.bfloat16).reshape(xsend.shape)
    get_q.wait()
    get_par.wait()
    for rr in order:
        src = z * TEAM + rr
        remote(qbuf.at[src], qbuf.at[src], q_send.at[0], q_recv.at[src], src).wait_recv()
        remote(par_ref, ptab.at[src], p_send.at[0], p_recv.at[src], src).wait_recv()

    @pl.when(core == 1)
    def _():
        pl.semaphore_wait(barrier, n - TEAM)
        tell(ready, z * TEAM + partner)

    @pl.when(core == 0)
    def _():
        pl.semaphore_wait(ready, 1)

    def shared(zz, to):
        block = pl.ds(zz * TEAM, TEAM)
        dev = to * TEAM + r
        return [remote(ptab.at[block], ptab.at[block], p_send.at[TEAM - 1 + to], pz_recv.at[zz], dev),
                remote(qbuf.at[block], qbuf.at[block], q_send.at[TEAM - 1 + to], qz_recv.at[zz], dev)]

    for zz in far_first:
        for cp in shared(z, zz):
            send(cp)
    own_x = pltpu.make_async_copy(xsend.at[me], xrecv.at[me], local_sem.at[6])
    own_x.start()

    def send_x(devs, at):
        for k, dev in enumerate(devs):
            send(remote(xsend.at[dev], xrecv.at[me], x_send.at[at + k], x_recv.at[me], dev))

    near = [(zz, rr) for zz in others for rr in (r, partner)] + [(z, partner)]
    across = [(zz, rr) for zz in range(depth) for rr in order[:2]]
    send_x([zz * TEAM + rr for zz, rr in near], 0)
    send_x([zz * TEAM + rr for zz, rr in across[:2]], len(near))

    for zz in others:
        shared(zz, zz)[0].wait_recv()
    table = jnp.concatenate([ptab[u] for u in range(utts)], axis=0)
    beam_lane = lax.broadcasted_iota(jnp.int32, table.shape, 1)
    slot = jnp.concatenate(
        [jnp.sum(jnp.where(beam_lane == b, table, 0), axis=1, keepdims=True) for b in range(n)], axis=0)
    slot = jnp.broadcast_to(slot - z * TEAM, (count, old))
    lane = lax.broadcasted_iota(jnp.int32, (count, old), 1)
    row_u = lax.rem(lax.broadcasted_iota(jnp.int32, (count, old), 0), utts)
    own_key = lane // history == row_u
    here = (slot[:, :1] >= 0) & (slot[:, :1] < TEAM)
    spot = lane - row_u

    get_new.wait()
    own = []
    for h in range(feature // HD):
        q = newbuf[:, h * HD : (h + 1) * HD].astype(jnp.float32)
        k = newbuf[:, feature + h * HD : feature + (h + 1) * HD].astype(jnp.float32)
        own.append(jnp.sum(q * k, axis=1, keepdims=True) * scale)

    for zz in others:
        shared(zz, zz)[1].wait_recv()

    def arrive(h, i):
        get_own[h][i].wait()
        buf = (kbuf, vbuf)[i]
        for rr in order:
            remote(buf.at[h, rr], buf.at[h, rr], c_send.at[2 * h + i, 0], c_recv.at[2 * h + i, rr],
                   z * TEAM + rr).wait_recv()

    team = across[:2] + near + across[2:]
    stats = jnp.zeros((count, HD), jnp.float32)
    weight = []

    def score(h):
        arrive(h, 0)
        q = qbuf[:, :, h * HD : (h + 1) * HD].reshape(count, HD)
        s = contract_last(q, kbuf[h].reshape(TEAM * old, HD))
        picked = s[:, :old]
        for t in range(1, TEAM):
            picked = jnp.where(slot == t, s[:, t * old : (t + 1) * old], picked)
        picked = jnp.where(own_key, picked * scale, LOW)
        m = jnp.max(picked, axis=1, keepdims=True)
        e = jnp.where(own_key, jnp.exp(picked - m), 0.0)
        total = jnp.sum(e, axis=1, keepdims=True)
        e = e * (1.0 / total)
        weight.append(jnp.concatenate(
            [jnp.where(slot == t, e, 0.0).astype(jnp.bfloat16) for t in range(TEAM)], axis=1))
        return jnp.where(spot == h * utts, jnp.where(here, m + jnp.log(total), 0.0), stats)

    def values(h, first, size):
        o = jnp.dot(weight[h][first * span : (first + size) * span], vbuf[h].reshape(TEAM * old, HD),
                    preferred_element_type=jnp.float32)
        ctx[h, first : first + size] = o.astype(jnp.bfloat16).reshape(size, TEAM, utts, HD)

    def give_back(h, picks):
        for k in picks:
            zz, rr = team[k]
            send(remote(ctx.at[h, zz, rr], gbuf.at[h, me], g_send.at[h, k], g_recv.at[h, me],
                        zz * TEAM + rr))

    span = TEAM * utts
    now = range(2 + len(near))
    later = range(2 + len(near), n - 1)
    held = []
    stats = score(0)
    for h in range(1, heads):
        if h == 1:
            arrive(0, 1)
            values(0, 0, depth)
            give_back(0, now)
            give_back(0, later) if False else held.append(0)
        stats = score(h)
    for g in range(n):
        sstat[g] = jnp.sum(stats[g * utts : (g + 1) * utts], axis=0, keepdims=True)
    for k, (zz, rr) in enumerate(team):
        send(remote(sstat.at[zz * TEAM + rr], gstat.at[me], s_send.at[k], s_recv.at[me], zz * TEAM + rr))
    for h in range(1, last):
        arrive(h, 1)
        values(h, 0, depth)
        give_back(h, now)
        give_back(h, later) if False else held.append(h)
    mark = len(sends)
    arrive(last, 1)
    values(last, 0, 1)
    give_back(last, range(2))
    values(last, 1, depth - 1)
    give_back(last, range(2, n - 1)[: len(now) - 2])
    for h in held:
        give_back(h, later)
    give_back(last, later)
    send_x([zz * TEAM + rr for zz, rr in across[2:]], len(near) + 2)
    for h in range(heads):
        gbuf[h, pl.ds(me, 1)] = ctx[h, pl.ds(z, 1), pl.ds(r, 1)].reshape(1, utts, HD)
    gstat[pl.ds(me, 1)] = sstat[pl.ds(me, 1)]

    own_x.wait()
    for k in range(1, n):
        src = lax.rem(me + n - k, n)
        remote(xsend.at[src], xrecv.at[src], x_send.at[0], x_recv.at[src], src).wait_recv()
    to_row = lax.broadcasted_iota(jnp.int32, (utts * count_h, utts * pad), 0)
    from_row = lax.broadcasted_iota(jnp.int32, (utts * count_h, utts * pad), 1)
    turn = (to_row % utts == from_row // pad) & (to_row // utts == from_row % pad)
    cross_ctx[...] = jnp.dot(turn.astype(jnp.bfloat16), xrecv[...].reshape(utts * pad, HD),
                             preferred_element_type=jnp.float32)

    for k in range(1, n):
        src = lax.rem(me + n - k, n)
        remote(gstat.at[src], gstat.at[src], s_send.at[0], s_recv.at[src], src).wait_recv()
    weights = []
    f_lane = lax.broadcasted_iota(jnp.int32, (utts, HD), 1)
    f_row = lax.broadcasted_iota(jnp.int32, (utts, HD), 0)
    for t in range(TEAM):
        packed = gstat[t]
        for zz in range(1, depth):
            packed = packed + gstat[zz * TEAM + t]
        packed = jnp.broadcast_to(packed, (utts, HD))
        for hl in range(heads):
            lse = jnp.sum(jnp.where(f_lane == f_row + hl * utts, packed, 0.0), axis=1, keepdims=True)
            mine = own[t * heads + hl]
            peak = jnp.maximum(lse, mine)
            w_old = jnp.exp(lse - peak)
            w_own = jnp.exp(mine - peak)
            inv = 1.0 / (w_old + w_own)
            weights.append((w_old * inv, w_own * inv))

    def write(t, hl):
        h = t * heads + hl
        hc = slice(h * HD, (h + 1) * HD)
        got = gbuf[hl, t]
        for zz in range(1, depth):
            got = got + gbuf[hl, zz * TEAM + t]
        w_old, w_own = weights[h]
        value = newbuf[:, 2 * feature + h * HD : 2 * feature + (h + 1) * HD].astype(jnp.float32)
        self_ctx = got.astype(jnp.float32) * w_old + value * w_own
        out_ref[:, hc] = (
            self_ctx.astype(jnp.bfloat16).astype(jnp.float32) + cross_ctx[h * utts : (h + 1) * utts]
        ).astype(jnp.bfloat16)

    for cp in sends[:mark]:
        cp.wait_send()
    for hl in range(heads):
        for k in range(1, n):
            src = lax.rem(me + n - k, n)
            remote(gbuf.at[hl, src], gbuf.at[hl, src], g_send.at[hl, 0], g_recv.at[hl, src], src).wait_recv()
        for t in range(TEAM):
            write(t, hl)

    for cp in sends[mark:]:
        cp.wait_send()


def fast_body(n, cache_kv, new_rows, cross_queries, enc_kv, lengths, parents):
    rows, feature = cross_queries.shape
    utts, history, width = cache_kv.shape
    old = utts * history
    depth = n // TEAM
    quarter = feature // TEAM
    heads = quarter // HD
    frames = enc_kv.shape[1]
    pad = -(-(feature // HD) // 8) * 8
    bf, f32 = jnp.bfloat16, jnp.float32
    dma = pltpu.SemaphoreType.DMA
    hbm = pl.BlockSpec(memory_space=pl.ANY)
    return pl.pallas_call(
        functools.partial(fast_kernel, n),
        out_shape=pltpu.VMEM((utts, feature), bf),
        in_specs=[hbm] * 6,
        out_specs=pl.BlockSpec(memory_space=pltpu.VMEM),
        scratch_shapes=[
            pltpu.VMEM((n, utts, quarter), bf),
            pltpu.VMEM((heads, TEAM, old, HD), bf),
            pltpu.VMEM((heads, TEAM, old, HD), bf),
            pltpu.VMEM(new_rows.shape, bf),
            pltpu.VMEM(cross_queries.shape, bf),
            pltpu.VMEM((frames, width), bf),
            pltpu.VMEM((n,) + parents.shape, jnp.int32),
            pltpu.VMEM((rows, pad, HD), bf),
            pltpu.VMEM((utts, pad, HD), bf),
            pltpu.VMEM((utts * (feature // HD), HD), f32),
            pltpu.VMEM((heads, depth, TEAM, utts, HD), bf),
            pltpu.VMEM((heads, n, utts, HD), bf),
            pltpu.VMEM((n, 1, HD), f32),
            pltpu.VMEM((n, 1, HD), f32),
            pltpu.SMEM(lengths.shape, jnp.int32),
            dma((7,)), dma((2 * heads,)), dma((TEAM - 1 + depth,)), dma((n,)), dma((depth,)),
            dma((TEAM - 1 + depth,)), dma((n,)), dma((depth,)),
            dma((2 * heads, TEAM - 1)), dma((2 * heads, TEAM)),
            dma((n - 1,)), dma((n,)), dma((n - 1,)), dma((n,)),
            dma((heads, n - 1)), dma((heads, n)), pltpu.SemaphoreType.REGULAR,
        ],
        compiler_params=pltpu.CompilerParams(
            collective_id=0, has_side_effects=True, vmem_limit_bytes=64 * 2**20 - 144 * 1024
        ),
    )(cache_kv.reshape(old, width), new_rows, cross_queries, enc_kv, lengths, parents)


def reorder(cache_rows, parents):
    utterances, beam_width = parents.shape
    grouped = cache_rows.reshape(utterances, beam_width, cache_rows.shape[1], cache_rows.shape[2])
    beams = lax.broadcasted_iota(jnp.int32, (1, 1, beam_width), 2)
    pick = (parents[:, :, None] == beams).astype(cache_rows.dtype)
    picked = jnp.einsum("ubp,uptc->ubtc", pick, grouped, preferred_element_type=jnp.float32)
    return picked.astype(cache_rows.dtype).reshape(cache_rows.shape)


def attend_self(query, old_keys, old_values, new_key, new_value):
    row_count = query.shape[0]
    history = old_keys.shape[1]
    head_count = query.shape[1] // HD
    scale = HD ** (-0.5)
    query_heads = query.reshape(row_count, head_count, HD)
    key_heads = old_keys.reshape(row_count, history, head_count, HD)
    value_heads = old_values.reshape(row_count, history, head_count, HD)
    old_scores = (
        jnp.einsum("rhd,rthd->rht", query_heads, key_heads, preferred_element_type=jnp.float32)
        * scale
    )
    own_score = (
        jnp.einsum(
            "rhd,rhd->rh",
            query_heads,
            new_key.reshape(row_count, head_count, HD),
            preferred_element_type=jnp.float32,
        )
        * scale
    )
    peak = jnp.maximum(jnp.max(old_scores, axis=2), own_score)
    old_exp = jnp.exp(old_scores - peak[:, :, None])
    own_exp = jnp.exp(own_score - peak)
    total = jnp.sum(old_exp, axis=2) + own_exp
    old_weight = (old_exp / total[:, :, None]).astype(jnp.bfloat16)
    own_weight = (own_exp / total).astype(jnp.bfloat16)
    context = jnp.einsum(
        "rht,rthd->rhd", old_weight, value_heads, preferred_element_type=jnp.float32
    )
    context = context + own_weight.astype(jnp.float32)[:, :, None] * new_value.reshape(
        row_count, head_count, HD
    ).astype(jnp.float32)
    return context.reshape(row_count, head_count * HD).astype(jnp.bfloat16)


def attend_frames(queries, frames_kv, frame_counts):
    utterances = frame_counts.shape[0]
    beam_width = queries.shape[0] // utterances
    feature = queries.shape[1]
    head_count = feature // HD
    frame_total = frames_kv.shape[1]
    scale = HD ** (-0.5)
    query_heads = queries.reshape(utterances, beam_width, head_count, HD)
    key_heads = frames_kv[:, :, :feature].reshape(utterances, frame_total, head_count, HD)
    value_heads = frames_kv[:, :, feature:].reshape(utterances, frame_total, head_count, HD)
    scores = (
        jnp.einsum("ubhd,ufhd->uhbf", query_heads, key_heads, preferred_element_type=jnp.float32)
        * scale
    )
    live = (
        lax.broadcasted_iota(jnp.int32, (utterances, 1, 1, frame_total), 3)
        < frame_counts[:, None, None, None]
    )
    scores = jnp.where(live, scores, -1e30)
    peak = jnp.max(scores, axis=3, keepdims=True)
    raised = jnp.where(live, jnp.exp(scores - peak), 0.0)
    weights = (raised / jnp.sum(raised, axis=3, keepdims=True)).astype(jnp.bfloat16)
    context = jnp.einsum(
        "uhbf,ufhd->ubhd", weights, value_heads, preferred_element_type=jnp.float32
    )
    return context.reshape(utterances * beam_width, feature)


def body(cache_kv, new_rows, cross_queries, enc_kv, lengths, parents):
    feature = cross_queries.shape[1]
    cross_context = attend_frames(cross_queries, enc_kv, lengths)
    arrived, new_here = (
        lax.all_to_all(cache_kv, "utt", split_axis=0, concat_axis=0, tiled=True),
        lax.all_to_all(new_rows, "utt", split_axis=0, concat_axis=0, tiled=True),
    )
    reordered = reorder(arrived, parents)
    self_context = attend_self(
        new_here[:, :feature],
        reordered[:, :, :feature],
        reordered[:, :, feature:],
        new_here[:, feature : 2 * feature],
        new_here[:, 2 * feature :],
    )
    mixed_here = (self_context.astype(jnp.float32) + cross_context).astype(jnp.bfloat16)
    mixed = lax.all_to_all(mixed_here, "utt", split_axis=0, concat_axis=0, tiled=True)
    return mixed


def solution(mesh):
    placed = (
        P(("groups", "utt"), None, None),
        P(("groups", "utt"), None),
        P(("groups", "utt"), None),
        P(("groups", "utt"), None, None),
        P(("groups", "utt")),
        P(("groups", "utt"), None),
    )
    n = mesh.shape["utt"]

    def either(cache_kv, new_rows, cross_queries, enc_kv, lengths, parents):
        feature = cross_queries.shape[1]
        fits = (
            parents.shape == (1, n)
            and cache_kv.shape[0] == n
            and n % TEAM == 0
            and n > TEAM
            and feature % (TEAM * HD) == 0
            and cache_kv.shape[0] * cache_kv.shape[1] == HD
            and feature // (TEAM * HD) * n <= HD
        )
        run = functools.partial(fast_body, n) if fits else body
        return run(cache_kv, new_rows, cross_queries, enc_kv, lengths, parents)

    return jax.shard_map(
        either, mesh=mesh, in_specs=placed, out_specs=P(("groups", "utt"), None), check_vma=False
    )
```

```python
import functools

import jax
import jax.numpy as jnp
from jax import lax
from jax.experimental import pallas as pl
from jax.experimental.pallas import tpu as pltpu
from jax.sharding import PartitionSpec as P

HD = 128
TEAM = 4
CORES = 2
LOW = -1e30


def contract_last(a, b):
    return lax.dot_general(a, b, (((1,), (1,)), ((), ())), preferred_element_type=jnp.float32)


def fast_kernel(
    n,
    cache_ref, new_ref, cq_ref, enc_ref, len_ref, par_ref,
    out_ref,
    qbuf, kbuf, vbuf, newbuf, cqbuf, encbuf, ptab, xsend, xrecv, cross_ctx,
    ctx, gbuf, sstat, gstat, len_smem,
    local_sem, own_sem, sent, got, c_recv, g_recv, ready,
):
    feature = cq_ref.shape[1]
    quarter = feature // TEAM
    heads = quarter // HD
    rows = cq_ref.shape[0]
    utts = new_ref.shape[0]
    old = cache_ref.shape[0]
    history = old // utts
    depth = n // TEAM
    count = n * utts
    scale = HD ** (-0.5)

    me = lax.axis_index("utt")
    z = me // TEAM
    r = me % TEAM
    others = [k + (k + depth - z) // depth for k in range(depth - 1)]
    upper = 2 * z // depth
    downward = [depth - 2 - k + (2 * depth - 2 - k - z) // depth for k in range(depth - 1)]
    far_first = [upper * a + (1 - upper) * b for a, b in zip(others, downward)]

    def remote(src, dst, ssem, rsem, dev):
        return pltpu.make_async_remote_copy(
            src_ref=src, dst_ref=dst, send_sem=ssem, recv_sem=rsem,
            device_id={"utt": dev}, device_id_type=pl.DeviceIdType.MESH,
        )

    core = r % CORES
    partner = r + 1 - 2 * core
    order = [lax.rem(r + CORES, TEAM), lax.rem(partner + CORES, TEAM), partner]

    def tell(sem, dev):
        pl.semaphore_signal(sem, inc=1, device_id={"utt": dev}, device_id_type=pl.DeviceIdType.MESH)

    barrier = pltpu.get_barrier_semaphore()
    tell(barrier, z * TEAM + lax.rem(r - core + CORES, TEAM))

    @pl.when(core == 1)
    def _():
        tell(barrier, z * TEAM + partner)

    for zz in others:
        for t in range(1, TEAM, CORES):
            tell(barrier, zz * TEAM + t)

    def cols(start, size):
        return pl.ds(pl.multiple_of(start, HD), size)

    get_len = pltpu.make_async_copy(len_ref, len_smem, local_sem.at[0])
    get_cq = pltpu.make_async_copy(cq_ref, cqbuf, local_sem.at[1])
    get_enc = pltpu.make_async_copy(enc_ref.at[0], encbuf, local_sem.at[2])
    get_new = pltpu.make_async_copy(new_ref, newbuf, local_sem.at[3])
    get_par = pltpu.make_async_copy(par_ref, ptab.at[me], local_sem.at[4])
    get_q = pltpu.make_async_copy(new_ref.at[:, cols(r * quarter, quarter)], qbuf.at[me], local_sem.at[5])
    for cp in (get_len, get_cq, get_enc, get_q, get_par, get_new):
        cp.start()
    for h in range(heads):
        for i, buf in enumerate((kbuf, vbuf)):
            pltpu.make_async_copy(
                cache_ref.at[:, cols(i * feature + r * quarter + h * HD, HD)], buf.at[h, r],
                own_sem.at[i]).start()

    frames = encbuf.shape[0]
    ones_f = jnp.ones((frames, HD), jnp.bfloat16)

    crossed = []

    def cross(h, live):
        hc = slice(h * HD, (h + 1) * HD)
        s = contract_last(cqbuf[:, hc], encbuf[:, hc]) * scale
        s = jnp.where(live, s, LOW)
        p = jnp.where(live, jnp.exp(s - jnp.max(s, axis=1, keepdims=True)), 0.0).astype(jnp.bfloat16)
        v = jnp.concatenate([encbuf[:, feature + h * HD : feature + (h + 1) * HD], ones_f], axis=1)
        o = jnp.dot(p, v, preferred_element_type=jnp.float32)
        crossed.append((o[:, :HD] / o[:, HD:]).astype(jnp.bfloat16))

    @pl.when(core == 0)
    def _():
        pl.semaphore_wait(barrier, TEAM - 1)
        tell(ready, z * TEAM + partner)

    @pl.when(core == 1)
    def _():
        pl.semaphore_wait(ready, 1)

    def send(src, dst, ssem, rsem, dev):
        remote(src, dst, sent.at[ssem], rsem, dev).start()

    def receive(ref, rsem):
        remote(ref, ref, sent.at[0], rsem, z * TEAM + partner).wait_recv()

    def drain(ref, ssem):
        remote(ref, ref, sent.at[ssem], got.at[0], z * TEAM + partner).wait_send()

    far = tuple(range(TEAM - 2))
    def ask(i):
        dev = z * TEAM + order[i]
        send(new_ref.at[:, cols(order[i] * quarter, quarter)], qbuf.at[me], 0, got.at[0], dev)
        send(par_ref, ptab.at[me], 1, got.at[1], dev)

    for i in range(TEAM - 1):
        ask(i)

    def give(h, i, js):
        buf = (kbuf, vbuf)[i]
        for j in js:
            send(cache_ref.at[:, cols(i * feature + order[j] * quarter + h * HD, HD)], buf.at[h, r],
                 2 + i, c_recv.at[2 * h + i], z * TEAM + order[j])

    last = heads - 1
    give(0, 0, far)
    give(0, 1, far)
    stream = [(h, i) for i in range(2) for h in range(1, heads)]
    if heads > 2:
        stream = [(1, 0), (2, 0), (1, 1), (2, 1)] + [(h, i) for h in range(3, heads) for i in range(2)]
    for h, i in stream:
        give(h, i, far)
    for h in range(heads):
        for i in range(2):
            give(h, i, (TEAM - 2,))

    get_len.wait()
    get_cq.wait()
    get_enc.wait()
    live = lax.broadcasted_iota(jnp.int32, (rows, frames), 1) < len_smem[0]
    count_h = feature // HD

    for h in range(count_h):
        cross(h, live)
    pad = xsend.shape[1]
    to_row = lax.broadcasted_iota(jnp.int32, (rows * pad, rows * count_h), 0)
    from_row = lax.broadcasted_iota(jnp.int32, (rows * pad, rows * count_h), 1)
    turn = (to_row // pad == from_row % rows) & (to_row % pad == from_row // rows)
    turned = jnp.dot(turn.astype(jnp.bfloat16), jnp.concatenate(crossed, axis=0),
                     preferred_element_type=jnp.float32)
    xsend[...] = turned.astype(jnp.bfloat16).reshape(xsend.shape)

    @pl.when(core == 1)
    def _():
        pl.semaphore_wait(barrier, n - TEAM)
        tell(ready, z * TEAM + partner)

    get_q.wait()
    get_par.wait()
    receive(qbuf.at[pl.ds(0, TEAM - 1)], got.at[0])
    receive(ptab.at[pl.ds(0, TEAM - 1)], got.at[1])

    @pl.when(core == 0)
    def _():
        pl.semaphore_wait(ready, 1)

    block = pl.ds(z * TEAM, TEAM)
    for zz in far_first:
        send(ptab.at[block], ptab.at[block], 1, got.at[3], zz * TEAM + r)
        send(qbuf.at[block], qbuf.at[block], 0, got.at[2], zz * TEAM + r)
    own_x = pltpu.make_async_copy(xsend.at[me], xrecv.at[me], local_sem.at[6])
    own_x.start()

    def send_x(picks):
        for zz, rr in picks:
            dev = zz * TEAM + rr
            send(xsend.at[dev], xrecv.at[me], 4, got.at[4], dev)

    near = [(zz, rr) for zz in others for rr in (r, partner)] + [(z, partner)]
    across = [(zz, rr) for zz in range(depth) for rr in order[:2]]
    send_x(near)
    send_x(across[:2])

    receive(ptab.at[pl.ds(0, n - TEAM)], got.at[3])
    table = jnp.concatenate([ptab[u] for u in range(utts)], axis=0)
    beam_lane = lax.broadcasted_iota(jnp.int32, table.shape, 1)
    slot = jnp.concatenate(
        [jnp.sum(jnp.where(beam_lane == b, table, 0), axis=1, keepdims=True) for b in range(n)], axis=0)
    slot = jnp.broadcast_to(slot - z * TEAM, (count, old))
    lane = lax.broadcasted_iota(jnp.int32, (count, old), 1)
    row_u = lax.rem(lax.broadcasted_iota(jnp.int32, (count, old), 0), utts)
    own_key = lane // history == row_u
    here = (slot[:, :1] >= 0) & (slot[:, :1] < TEAM)
    spot = lane - row_u

    get_new.wait()
    own = []
    for h in range(feature // HD):
        q = newbuf[:, h * HD : (h + 1) * HD].astype(jnp.float32)
        k = newbuf[:, feature + h * HD : feature + (h + 1) * HD].astype(jnp.float32)
        own.append(jnp.sum(q * k, axis=1, keepdims=True) * scale)

    receive(qbuf.at[pl.ds(0, n - TEAM)], got.at[2])

    def arrive(h, i):
        buf = (kbuf, vbuf)[i]
        if h == 0:
            mine = buf.at[:, pl.ds(r, 1)]
            pltpu.make_async_copy(mine, mine, own_sem.at[i]).wait()
        receive(buf.at[h, pl.ds(0, TEAM - 1)], c_recv.at[2 * h + i])

    team = across[:2] + near + across[2:]
    stats = jnp.zeros((count, HD), jnp.float32)
    weight = []

    def score(h):
        arrive(h, 0)
        q = qbuf[:, :, h * HD : (h + 1) * HD].reshape(count, HD)
        s = contract_last(q, kbuf[h].reshape(TEAM * old, HD))
        picked = s[:, :old]
        for t in range(1, TEAM):
            picked = jnp.where(slot == t, s[:, t * old : (t + 1) * old], picked)
        picked = jnp.where(own_key, picked * scale, LOW)
        m = jnp.max(picked, axis=1, keepdims=True)
        e = jnp.where(own_key, jnp.exp(picked - m), 0.0)
        total = jnp.sum(e, axis=1, keepdims=True)
        e = e * (1.0 / total)
        weight.append(jnp.concatenate(
            [jnp.where(slot == t, e, 0.0).astype(jnp.bfloat16) for t in range(TEAM)], axis=1))
        return jnp.where(spot == h * utts, jnp.where(here, m + jnp.log(total), 0.0), stats)

    def values(h, first, size):
        o = jnp.dot(weight[h][first * span : (first + size) * span], vbuf[h].reshape(TEAM * old, HD),
                    preferred_element_type=jnp.float32)
        ctx[h, first : first + size] = o.astype(jnp.bfloat16).reshape(size, TEAM, utts, HD)

    def give_back(h, picks):
        for k in picks:
            zz, rr = team[k]
            send(ctx.at[h, zz, rr], gbuf.at[h, me], 5, g_recv.at[h], zz * TEAM + rr)

    span = TEAM * utts
    now = range(2 + len(near))
    later = range(2 + len(near), n - 1)
    held = []
    stats = score(0)
    for h in range(1, heads):
        if h == 1:
            arrive(0, 1)
            values(0, 0, depth)
            give_back(0, now)
            held.append(0)
        stats = score(h)
    for g in range(n):
        sstat[g] = jnp.sum(stats[g * utts : (g + 1) * utts], axis=0, keepdims=True)
    for zz, rr in team:
        send(sstat.at[zz * TEAM + rr], gstat.at[me], 6, got.at[5], zz * TEAM + rr)
    for h in range(1, last):
        arrive(h, 1)
        values(h, 0, depth)
        give_back(h, now)
        held.append(h)
    arrive(last, 1)
    values(last, 0, 1)
    give_back(last, range(2))
    values(last, 1, depth - 1)
    give_back(last, range(2, 2 + len(near)))
    send_x(across[2:])
    for h in held:
        give_back(h, later)
    give_back(last, later)
    for h in range(heads):
        gbuf[h, pl.ds(me, 1)] = ctx[h, pl.ds(z, 1), pl.ds(r, 1)].reshape(1, utts, HD)
    gstat[pl.ds(me, 1)] = sstat[pl.ds(me, 1)]

    own_x.wait()
    receive(xrecv.at[pl.ds(0, n - 1)], got.at[4])
    to_row = lax.broadcasted_iota(jnp.int32, (utts * count_h, utts * pad), 0)
    from_row = lax.broadcasted_iota(jnp.int32, (utts * count_h, utts * pad), 1)
    turn = (to_row % utts == from_row // pad) & (to_row // utts == from_row % pad)
    cross_ctx[...] = jnp.dot(turn.astype(jnp.bfloat16), xrecv[...].reshape(utts * pad, HD),
                             preferred_element_type=jnp.float32)

    receive(gstat.at[pl.ds(0, n - 1)], got.at[5])
    weights = []
    f_lane = lax.broadcasted_iota(jnp.int32, (utts, HD), 1)
    f_row = lax.broadcasted_iota(jnp.int32, (utts, HD), 0)
    for t in range(TEAM):
        packed = gstat[t]
        for zz in range(1, depth):
            packed = packed + gstat[zz * TEAM + t]
        packed = jnp.broadcast_to(packed, (utts, HD))
        for hl in range(heads):
            lse = jnp.sum(jnp.where(f_lane == f_row + hl * utts, packed, 0.0), axis=1, keepdims=True)
            mine = own[t * heads + hl]
            peak = jnp.maximum(lse, mine)
            w_old = jnp.exp(lse - peak)
            w_own = jnp.exp(mine - peak)
            inv = 1.0 / (w_old + w_own)
            weights.append((w_old * inv, w_own * inv))

    def write(t, hl):
        h = t * heads + hl
        hc = slice(h * HD, (h + 1) * HD)
        got = gbuf[hl, t]
        for zz in range(1, depth):
            got = got + gbuf[hl, zz * TEAM + t]
        w_old, w_own = weights[h]
        value = newbuf[:, 2 * feature + h * HD : 2 * feature + (h + 1) * HD].astype(jnp.float32)
        self_ctx = got.astype(jnp.float32) * w_old + value * w_own
        out_ref[:, hc] = (
            self_ctx.astype(jnp.bfloat16).astype(jnp.float32) + cross_ctx[h * utts : (h + 1) * utts]
        ).astype(jnp.bfloat16)

    most = pl.ds(0, n - 1)
    for hl in range(heads):
        if hl == last:
            drain(qbuf.at[most], 0)
            drain(ptab.at[most], 1)
            drain(kbuf.at[:, pl.ds(0, TEAM - 1)], 2)
            drain(vbuf.at[:, pl.ds(0, TEAM - 1)], 3)
            drain(xrecv.at[most], 4)
            drain(gbuf.at[:, most], 5)
            drain(gstat.at[most], 6)
        receive(gbuf.at[hl, most], g_recv.at[hl])
        for t in range(TEAM):
            write(t, hl)


def fast_body(n, cache_kv, new_rows, cross_queries, enc_kv, lengths, parents):
    rows, feature = cross_queries.shape
    utts, history, width = cache_kv.shape
    old = utts * history
    depth = n // TEAM
    quarter = feature // TEAM
    heads = quarter // HD
    frames = enc_kv.shape[1]
    pad = -(-(feature // HD) // 8) * 8
    bf, f32 = jnp.bfloat16, jnp.float32
    dma = pltpu.SemaphoreType.DMA
    hbm = pl.BlockSpec(memory_space=pl.ANY)
    return pl.pallas_call(
        functools.partial(fast_kernel, n),
        out_shape=pltpu.VMEM((utts, feature), bf),
        in_specs=[hbm] * 6,
        out_specs=pl.BlockSpec(memory_space=pltpu.VMEM),
        scratch_shapes=[
            pltpu.VMEM((n, utts, quarter), bf),
            pltpu.VMEM((heads, TEAM, old, HD), bf),
            pltpu.VMEM((heads, TEAM, old, HD), bf),
            pltpu.VMEM(new_rows.shape, bf),
            pltpu.VMEM(cross_queries.shape, bf),
            pltpu.VMEM((frames, width), bf),
            pltpu.VMEM((n,) + parents.shape, jnp.int32),
            pltpu.VMEM((rows, pad, HD), bf),
            pltpu.VMEM((utts, pad, HD), bf),
            pltpu.VMEM((utts * (feature // HD), HD), f32),
            pltpu.VMEM((heads, depth, TEAM, utts, HD), bf),
            pltpu.VMEM((heads, n, utts, HD), bf),
            pltpu.VMEM((n, 1, HD), f32),
            pltpu.VMEM((n, 1, HD), f32),
            pltpu.SMEM(lengths.shape, jnp.int32),
            dma((7,)), dma((2,)), dma((7,)), dma((6,)), dma((2 * heads,)), dma((heads,)),
            pltpu.SemaphoreType.REGULAR,
        ],
        compiler_params=pltpu.CompilerParams(
            collective_id=0, has_side_effects=True, vmem_limit_bytes=64 * 2**20 - 144 * 1024
        ),
    )(cache_kv.reshape(old, width), new_rows, cross_queries, enc_kv, lengths, parents)


def reorder(cache_rows, parents):
    utterances, beam_width = parents.shape
    grouped = cache_rows.reshape(utterances, beam_width, cache_rows.shape[1], cache_rows.shape[2])
    beams = lax.broadcasted_iota(jnp.int32, (1, 1, beam_width), 2)
    pick = (parents[:, :, None] == beams).astype(cache_rows.dtype)
    picked = jnp.einsum("ubp,uptc->ubtc", pick, grouped, preferred_element_type=jnp.float32)
    return picked.astype(cache_rows.dtype).reshape(cache_rows.shape)


def attend_self(query, old_keys, old_values, new_key, new_value):
    row_count = query.shape[0]
    history = old_keys.shape[1]
    head_count = query.shape[1] // HD
    scale = HD ** (-0.5)
    query_heads = query.reshape(row_count, head_count, HD)
    key_heads = old_keys.reshape(row_count, history, head_count, HD)
    value_heads = old_values.reshape(row_count, history, head_count, HD)
    old_scores = (
        jnp.einsum("rhd,rthd->rht", query_heads, key_heads, preferred_element_type=jnp.float32)
        * scale
    )
    own_score = (
        jnp.einsum(
            "rhd,rhd->rh",
            query_heads,
            new_key.reshape(row_count, head_count, HD),
            preferred_element_type=jnp.float32,
        )
        * scale
    )
    peak = jnp.maximum(jnp.max(old_scores, axis=2), own_score)
    old_exp = jnp.exp(old_scores - peak[:, :, None])
    own_exp = jnp.exp(own_score - peak)
    total = jnp.sum(old_exp, axis=2) + own_exp
    old_weight = (old_exp / total[:, :, None]).astype(jnp.bfloat16)
    own_weight = (own_exp / total).astype(jnp.bfloat16)
    context = jnp.einsum(
        "rht,rthd->rhd", old_weight, value_heads, preferred_element_type=jnp.float32
    )
    context = context + own_weight.astype(jnp.float32)[:, :, None] * new_value.reshape(
        row_count, head_count, HD
    ).astype(jnp.float32)
    return context.reshape(row_count, head_count * HD).astype(jnp.bfloat16)


def attend_frames(queries, frames_kv, frame_counts):
    utterances = frame_counts.shape[0]
    beam_width = queries.shape[0] // utterances
    feature = queries.shape[1]
    head_count = feature // HD
    frame_total = frames_kv.shape[1]
    scale = HD ** (-0.5)
    query_heads = queries.reshape(utterances, beam_width, head_count, HD)
    key_heads = frames_kv[:, :, :feature].reshape(utterances, frame_total, head_count, HD)
    value_heads = frames_kv[:, :, feature:].reshape(utterances, frame_total, head_count, HD)
    scores = (
        jnp.einsum("ubhd,ufhd->uhbf", query_heads, key_heads, preferred_element_type=jnp.float32)
        * scale
    )
    live = (
        lax.broadcasted_iota(jnp.int32, (utterances, 1, 1, frame_total), 3)
        < frame_counts[:, None, None, None]
    )
    scores = jnp.where(live, scores, -1e30)
    peak = jnp.max(scores, axis=3, keepdims=True)
    raised = jnp.where(live, jnp.exp(scores - peak), 0.0)
    weights = (raised / jnp.sum(raised, axis=3, keepdims=True)).astype(jnp.bfloat16)
    context = jnp.einsum(
        "uhbf,ufhd->ubhd", weights, value_heads, preferred_element_type=jnp.float32
    )
    return context.reshape(utterances * beam_width, feature)


def body(cache_kv, new_rows, cross_queries, enc_kv, lengths, parents):
    feature = cross_queries.shape[1]
    cross_context = attend_frames(cross_queries, enc_kv, lengths)
    arrived, new_here = (
        lax.all_to_all(cache_kv, "utt", split_axis=0, concat_axis=0, tiled=True),
        lax.all_to_all(new_rows, "utt", split_axis=0, concat_axis=0, tiled=True),
    )
    reordered = reorder(arrived, parents)
    self_context = attend_self(
        new_here[:, :feature],
        reordered[:, :, :feature],
        reordered[:, :, feature:],
        new_here[:, feature : 2 * feature],
        new_here[:, 2 * feature :],
    )
    mixed_here = (self_context.astype(jnp.float32) + cross_context).astype(jnp.bfloat16)
    mixed = lax.all_to_all(mixed_here, "utt", split_axis=0, concat_axis=0, tiled=True)
    return mixed


def solution(mesh):
    placed = (
        P(("groups", "utt"), None, None),
        P(("groups", "utt"), None),
        P(("groups", "utt"), None),
        P(("groups", "utt"), None, None),
        P(("groups", "utt")),
        P(("groups", "utt"), None),
    )
    n = mesh.shape["utt"]

    def either(cache_kv, new_rows, cross_queries, enc_kv, lengths, parents):
        feature = cross_queries.shape[1]
        fits = (
            parents.shape == (1, n)
            and cache_kv.shape[0] == n
            and n % TEAM == 0
            and n > TEAM
            and feature % (TEAM * HD) == 0
            and cache_kv.shape[0] * cache_kv.shape[1] == HD
            and feature // (TEAM * HD) * n <= HD
        )
        run = functools.partial(fast_body, n) if fits else body
        return run(cache_kv, new_rows, cross_queries, enc_kv, lengths, parents)

    return jax.shard_map(
        either, mesh=mesh, in_specs=placed, out_specs=P(("groups", "utt"), None), check_vma=False
    )
```

```python
import functools

import jax
import jax.numpy as jnp
from jax import lax
from jax.experimental import pallas as pl
from jax.experimental.pallas import tpu as pltpu
from jax.sharding import PartitionSpec as P

HD = 128
TEAM = 4
CORES = 2
LOW = -1e30


def contract_last(a, b):
    return lax.dot_general(a, b, (((1,), (1,)), ((), ())), preferred_element_type=jnp.float32)


def fast_kernel(
    n,
    cache_ref, new_ref, cq_ref, enc_ref, len_ref, par_ref,
    out_ref,
    qbuf, kbuf, vbuf, newbuf, cqbuf, encbuf, ptab, xsend, xrecv, cross_ctx,
    ctx, gbuf, sstat, gstat, len_smem,
    local_sem, own_sem, sent, got, c_recv, g_recv, ready,
):
    feature = cq_ref.shape[1]
    quarter = feature // TEAM
    heads = quarter // HD
    rows = cq_ref.shape[0]
    utts = new_ref.shape[0]
    old = cache_ref.shape[0]
    history = old // utts
    depth = n // TEAM
    count = n * utts
    scale = HD ** (-0.5)

    me = lax.axis_index("utt")
    z = me // TEAM
    r = me % TEAM
    others = [k + (k + depth - z) // depth for k in range(depth - 1)]
    upper = 2 * z // depth
    downward = [depth - 2 - k + (2 * depth - 2 - k - z) // depth for k in range(depth - 1)]
    far_first = [upper * a + (1 - upper) * b for a, b in zip(others, downward)]

    def remote(src, dst, ssem, rsem, dev):
        return pltpu.make_async_remote_copy(
            src_ref=src, dst_ref=dst, send_sem=ssem, recv_sem=rsem,
            device_id={"utt": dev}, device_id_type=pl.DeviceIdType.MESH,
        )

    core = r % CORES
    partner = r + 1 - 2 * core
    order = [lax.rem(r + CORES, TEAM), lax.rem(partner + CORES, TEAM), partner]

    def tell(sem, dev):
        pl.semaphore_signal(sem, inc=1, device_id={"utt": dev}, device_id_type=pl.DeviceIdType.MESH)

    barrier = pltpu.get_barrier_semaphore()
    tell(barrier, z * TEAM + lax.rem(r - core + CORES, TEAM))

    @pl.when(core == 1)
    def _():
        tell(barrier, z * TEAM + partner)

    @pl.when(upper == 1)
    def _():
        tell(barrier, z * TEAM + lax.rem(r - core + 1 + CORES, TEAM))

    @pl.when(upper * (1 - core) == 1)
    def _():
        tell(barrier, z * TEAM + partner)

    for zz in others:
        for t in range(1, TEAM, CORES):
            tell(barrier, zz * TEAM + t)

    def cols(start, size):
        return pl.ds(pl.multiple_of(start, HD), size)

    get_len = pltpu.make_async_copy(len_ref, len_smem, local_sem.at[0])
    get_cq = pltpu.make_async_copy(cq_ref, cqbuf, local_sem.at[1])
    get_enc = pltpu.make_async_copy(enc_ref.at[0], encbuf, local_sem.at[2])
    get_new = pltpu.make_async_copy(new_ref, newbuf, local_sem.at[3])
    get_par = pltpu.make_async_copy(par_ref, ptab.at[me], local_sem.at[4])
    get_q = pltpu.make_async_copy(new_ref.at[:, cols(r * quarter, quarter)], qbuf.at[me], local_sem.at[5])
    for cp in (get_len, get_cq, get_enc, get_q, get_par, get_new):
        cp.start()
    for h in range(heads):
        for i, buf in enumerate((kbuf, vbuf)):
            pltpu.make_async_copy(
                cache_ref.at[:, cols(i * feature + r * quarter + h * HD, HD)], buf.at[h, r],
                own_sem.at[i]).start()

    frames = encbuf.shape[0]
    ones_f = jnp.ones((frames, HD), jnp.bfloat16)

    crossed = []

    def cross(h, live):
        hc = slice(h * HD, (h + 1) * HD)
        s = contract_last(cqbuf[:, hc], encbuf[:, hc]) * scale
        s = jnp.where(live, s, LOW)
        p = jnp.where(live, jnp.exp(s - jnp.max(s, axis=1, keepdims=True)), 0.0).astype(jnp.bfloat16)
        v = jnp.concatenate([encbuf[:, feature + h * HD : feature + (h + 1) * HD], ones_f], axis=1)
        o = jnp.dot(p, v, preferred_element_type=jnp.float32)
        crossed.append((o[:, :HD] / o[:, HD:]).astype(jnp.bfloat16))

    @pl.when(core == 0)
    def _():
        pl.semaphore_wait(barrier, TEAM - 1)

        @pl.when(upper == 0)
        def _():
            tell(ready, z * TEAM + partner)

    @pl.when(core * (1 - upper) == 1)
    def _():
        pl.semaphore_wait(ready, 1)

    @pl.when(core * upper == 1)
    def _():
        pl.semaphore_wait(barrier, n - 1)
        tell(ready, z * TEAM + partner)

    def send(src, dst, ssem, rsem, dev):
        remote(src, dst, sent.at[ssem], rsem, dev).start()

    def receive(ref, rsem):
        remote(ref, ref, sent.at[0], rsem, z * TEAM + partner).wait_recv()

    def drain(ref, ssem):
        remote(ref, ref, sent.at[ssem], got.at[0], z * TEAM + partner).wait_send()

    far = tuple(range(TEAM - 2))
    def ask(i):
        dev = z * TEAM + order[i]
        send(new_ref.at[:, cols(order[i] * quarter, quarter)], qbuf.at[me], 0, got.at[0], dev)
        send(par_ref, ptab.at[me], 1, got.at[1], dev)

    for i in range(TEAM - 1):
        ask(i)

    def give(h, i, js):
        buf = (kbuf, vbuf)[i]
        for j in js:
            send(cache_ref.at[:, cols(i * feature + order[j] * quarter + h * HD, HD)], buf.at[h, r],
                 2 + i, c_recv.at[2 * h + i], z * TEAM + order[j])

    last = heads - 1
    give(0, 0, far)
    give(0, 1, far)
    stream = [(h, i) for i in range(2) for h in range(1, heads)]
    if heads > 2:
        stream = [(1, 0), (2, 0), (1, 1), (2, 1)] + [(h, i) for h in range(3, heads) for i in range(2)]
    for h, i in stream:
        give(h, i, far)
    for h in range(heads):
        for i in range(2):
            give(h, i, (TEAM - 2,))

    get_len.wait()
    get_cq.wait()
    get_enc.wait()
    live = lax.broadcasted_iota(jnp.int32, (rows, frames), 1) < len_smem[0]
    count_h = feature // HD

    for h in range(count_h):
        cross(h, live)
    pad = xsend.shape[1]
    to_row = lax.broadcasted_iota(jnp.int32, (rows * pad, rows * count_h), 0)
    from_row = lax.broadcasted_iota(jnp.int32, (rows * pad, rows * count_h), 1)
    turn = (to_row // pad == from_row % rows) & (to_row % pad == from_row // rows)
    turned = jnp.dot(turn.astype(jnp.bfloat16), jnp.concatenate(crossed, axis=0),
                     preferred_element_type=jnp.float32)
    xsend[...] = turned.astype(jnp.bfloat16).reshape(xsend.shape)

    @pl.when(core * (1 - upper) == 1)
    def _():
        pl.semaphore_wait(barrier, n - TEAM)
        tell(ready, z * TEAM + partner)

    get_q.wait()
    get_par.wait()
    receive(qbuf.at[pl.ds(0, TEAM - 1)], got.at[0])
    receive(ptab.at[pl.ds(0, TEAM - 1)], got.at[1])

    @pl.when(core == 0)
    def _():
        pl.semaphore_wait(ready, 1)

    block = pl.ds(z * TEAM, TEAM)
    for zz in far_first:
        send(ptab.at[block], ptab.at[block], 1, got.at[3], zz * TEAM + r)
        send(qbuf.at[block], qbuf.at[block], 0, got.at[2], zz * TEAM + r)
    own_x = pltpu.make_async_copy(xsend.at[me], xrecv.at[me], local_sem.at[6])
    own_x.start()

    def send_x(picks):
        for zz, rr in picks:
            dev = zz * TEAM + rr
            send(xsend.at[dev], xrecv.at[me], 4, got.at[4], dev)

    near = [(zz, rr) for zz in others for rr in (r, partner)] + [(z, partner)]
    across = [(zz, rr) for zz in range(depth) for rr in order[:2]]
    send_x(near)
    send_x(across[:2])

    receive(ptab.at[pl.ds(0, n - TEAM)], got.at[3])
    table = jnp.concatenate([ptab[u] for u in range(utts)], axis=0)
    beam_lane = lax.broadcasted_iota(jnp.int32, table.shape, 1)
    slot = jnp.concatenate(
        [jnp.sum(jnp.where(beam_lane == b, table, 0), axis=1, keepdims=True) for b in range(n)], axis=0)
    slot = jnp.broadcast_to(slot - z * TEAM, (count, old))
    lane = lax.broadcasted_iota(jnp.int32, (count, old), 1)
    row_u = lax.rem(lax.broadcasted_iota(jnp.int32, (count, old), 0), utts)
    own_key = lane // history == row_u
    here = (slot[:, :1] >= 0) & (slot[:, :1] < TEAM)
    spot = lane - row_u

    get_new.wait()
    own = []
    for h in range(feature // HD):
        q = newbuf[:, h * HD : (h + 1) * HD].astype(jnp.float32)
        k = newbuf[:, feature + h * HD : feature + (h + 1) * HD].astype(jnp.float32)
        own.append(jnp.sum(q * k, axis=1, keepdims=True) * scale)

    receive(qbuf.at[pl.ds(0, n - TEAM)], got.at[2])

    def arrive(h, i):
        buf = (kbuf, vbuf)[i]
        if h == 0:
            mine = buf.at[:, pl.ds(r, 1)]
            pltpu.make_async_copy(mine, mine, own_sem.at[i]).wait()
        receive(buf.at[h, pl.ds(0, TEAM - 1)], c_recv.at[2 * h + i])

    team = across[:2] + near + across[2:]
    stats = jnp.zeros((count, HD), jnp.float32)
    weight = []

    def score(h):
        arrive(h, 0)
        q = qbuf[:, :, h * HD : (h + 1) * HD].reshape(count, HD)
        s = contract_last(q, kbuf[h].reshape(TEAM * old, HD))
        picked = s[:, :old]
        for t in range(1, TEAM):
            picked = jnp.where(slot == t, s[:, t * old : (t + 1) * old], picked)
        picked = jnp.where(own_key, picked * scale, LOW)
        m = jnp.max(picked, axis=1, keepdims=True)
        e = jnp.where(own_key, jnp.exp(picked - m), 0.0)
        total = jnp.sum(e, axis=1, keepdims=True)
        e = e * (1.0 / total)
        weight.append(jnp.concatenate(
            [jnp.where(slot == t, e, 0.0).astype(jnp.bfloat16) for t in range(TEAM)], axis=1))
        return jnp.where(spot == h * utts, jnp.where(here, m + jnp.log(total), 0.0), stats)

    def values(h, first, size):
        o = jnp.dot(weight[h][first * span : (first + size) * span], vbuf[h].reshape(TEAM * old, HD),
                    preferred_element_type=jnp.float32)
        ctx[h, first : first + size] = o.astype(jnp.bfloat16).reshape(size, TEAM, utts, HD)

    def give_back(h, picks):
        for k in picks:
            zz, rr = team[k]
            send(ctx.at[h, zz, rr], gbuf.at[h, me], 5, g_recv.at[h], zz * TEAM + rr)

    span = TEAM * utts
    now = range(2 + len(near))
    later = range(2 + len(near), n - 1)
    held = []
    stats = score(0)
    for h in range(1, heads):
        if h == 1:
            arrive(0, 1)
            values(0, 0, depth)
            give_back(0, now)
            held.append(0)
        stats = score(h)
    for g in range(n):
        sstat[g] = jnp.sum(stats[g * utts : (g + 1) * utts], axis=0, keepdims=True)
    for zz, rr in team:
        send(sstat.at[zz * TEAM + rr], gstat.at[me], 6, got.at[5], zz * TEAM + rr)
    for h in range(1, last):
        arrive(h, 1)
        values(h, 0, depth)
        give_back(h, now)
        held.append(h)
    arrive(last, 1)
    values(last, 0, 1)
    give_back(last, range(2))
    values(last, 1, depth - 1)
    give_back(last, range(2, 2 + len(near)))
    send_x(across[2:])
    for h in held:
        give_back(h, later)
    give_back(last, later)
    for h in range(heads):
        gbuf[h, pl.ds(me, 1)] = ctx[h, pl.ds(z, 1), pl.ds(r, 1)].reshape(1, utts, HD)
    gstat[pl.ds(me, 1)] = sstat[pl.ds(me, 1)]

    own_x.wait()
    receive(xrecv.at[pl.ds(0, n - 1)], got.at[4])
    to_row = lax.broadcasted_iota(jnp.int32, (utts * count_h, utts * pad), 0)
    from_row = lax.broadcasted_iota(jnp.int32, (utts * count_h, utts * pad), 1)
    turn = (to_row % utts == from_row // pad) & (to_row // utts == from_row % pad)
    cross_ctx[...] = jnp.dot(turn.astype(jnp.bfloat16), xrecv[...].reshape(utts * pad, HD),
                             preferred_element_type=jnp.float32)

    receive(gstat.at[pl.ds(0, n - 1)], got.at[5])
    weights = []
    f_lane = lax.broadcasted_iota(jnp.int32, (utts, HD), 1)
    f_row = lax.broadcasted_iota(jnp.int32, (utts, HD), 0)
    for t in range(TEAM):
        packed = gstat[t]
        for zz in range(1, depth):
            packed = packed + gstat[zz * TEAM + t]
        packed = jnp.broadcast_to(packed, (utts, HD))
        for hl in range(heads):
            lse = jnp.sum(jnp.where(f_lane == f_row + hl * utts, packed, 0.0), axis=1, keepdims=True)
            mine = own[t * heads + hl]
            peak = jnp.maximum(lse, mine)
            w_old = jnp.exp(lse - peak)
            w_own = jnp.exp(mine - peak)
            inv = 1.0 / (w_old + w_own)
            weights.append((w_old * inv, w_own * inv))

    def write(t, hl):
        h = t * heads + hl
        hc = slice(h * HD, (h + 1) * HD)
        got = gbuf[hl, t]
        for zz in range(1, depth):
            got = got + gbuf[hl, zz * TEAM + t]
        w_old, w_own = weights[h]
        value = newbuf[:, 2 * feature + h * HD : 2 * feature + (h + 1) * HD].astype(jnp.float32)
        self_ctx = got.astype(jnp.float32) * w_old + value * w_own
        out_ref[:, hc] = (
            self_ctx.astype(jnp.bfloat16).astype(jnp.float32) + cross_ctx[h * utts : (h + 1) * utts]
        ).astype(jnp.bfloat16)

    most = pl.ds(0, n - 1)
    for hl in range(heads):
        if hl == last:
            drain(qbuf.at[most], 0)
            drain(ptab.at[most], 1)
            drain(kbuf.at[:, pl.ds(0, TEAM - 1)], 2)
            drain(vbuf.at[:, pl.ds(0, TEAM - 1)], 3)
            drain(xrecv.at[most], 4)
            drain(gbuf.at[:, most], 5)
            drain(gstat.at[most], 6)
        receive(gbuf.at[hl, most], g_recv.at[hl])
        for t in range(TEAM):
            write(t, hl)


def fast_body(n, cache_kv, new_rows, cross_queries, enc_kv, lengths, parents):
    rows, feature = cross_queries.shape
    utts, history, width = cache_kv.shape
    old = utts * history
    depth = n // TEAM
    quarter = feature // TEAM
    heads = quarter // HD
    frames = enc_kv.shape[1]
    pad = -(-(feature // HD) // 8) * 8
    bf, f32 = jnp.bfloat16, jnp.float32
    dma = pltpu.SemaphoreType.DMA
    hbm = pl.BlockSpec(memory_space=pl.ANY)
    return pl.pallas_call(
        functools.partial(fast_kernel, n),
        out_shape=pltpu.VMEM((utts, feature), bf),
        in_specs=[hbm] * 6,
        out_specs=pl.BlockSpec(memory_space=pltpu.VMEM),
        scratch_shapes=[
            pltpu.VMEM((n, utts, quarter), bf),
            pltpu.VMEM((heads, TEAM, old, HD), bf),
            pltpu.VMEM((heads, TEAM, old, HD), bf),
            pltpu.VMEM(new_rows.shape, bf),
            pltpu.VMEM(cross_queries.shape, bf),
            pltpu.VMEM((frames, width), bf),
            pltpu.VMEM((n,) + parents.shape, jnp.int32),
            pltpu.VMEM((rows, pad, HD), bf),
            pltpu.VMEM((utts, pad, HD), bf),
            pltpu.VMEM((utts * (feature // HD), HD), f32),
            pltpu.VMEM((heads, depth, TEAM, utts, HD), bf),
            pltpu.VMEM((heads, n, utts, HD), bf),
            pltpu.VMEM((n, 1, HD), f32),
            pltpu.VMEM((n, 1, HD), f32),
            pltpu.SMEM(lengths.shape, jnp.int32),
            dma((7,)), dma((2,)), dma((7,)), dma((6,)), dma((2 * heads,)), dma((heads,)),
            pltpu.SemaphoreType.REGULAR,
        ],
        compiler_params=pltpu.CompilerParams(
            collective_id=0, has_side_effects=True, vmem_limit_bytes=64 * 2**20 - 144 * 1024
        ),
    )(cache_kv.reshape(old, width), new_rows, cross_queries, enc_kv, lengths, parents)


def reorder(cache_rows, parents):
    utterances, beam_width = parents.shape
    grouped = cache_rows.reshape(utterances, beam_width, cache_rows.shape[1], cache_rows.shape[2])
    beams = lax.broadcasted_iota(jnp.int32, (1, 1, beam_width), 2)
    pick = (parents[:, :, None] == beams).astype(cache_rows.dtype)
    picked = jnp.einsum("ubp,uptc->ubtc", pick, grouped, preferred_element_type=jnp.float32)
    return picked.astype(cache_rows.dtype).reshape(cache_rows.shape)


def attend_self(query, old_keys, old_values, new_key, new_value):
    row_count = query.shape[0]
    history = old_keys.shape[1]
    head_count = query.shape[1] // HD
    scale = HD ** (-0.5)
    query_heads = query.reshape(row_count, head_count, HD)
    key_heads = old_keys.reshape(row_count, history, head_count, HD)
    value_heads = old_values.reshape(row_count, history, head_count, HD)
    old_scores = (
        jnp.einsum("rhd,rthd->rht", query_heads, key_heads, preferred_element_type=jnp.float32)
        * scale
    )
    own_score = (
        jnp.einsum(
            "rhd,rhd->rh",
            query_heads,
            new_key.reshape(row_count, head_count, HD),
            preferred_element_type=jnp.float32,
        )
        * scale
    )
    peak = jnp.maximum(jnp.max(old_scores, axis=2), own_score)
    old_exp = jnp.exp(old_scores - peak[:, :, None])
    own_exp = jnp.exp(own_score - peak)
    total = jnp.sum(old_exp, axis=2) + own_exp
    old_weight = (old_exp / total[:, :, None]).astype(jnp.bfloat16)
    own_weight = (own_exp / total).astype(jnp.bfloat16)
    context = jnp.einsum(
        "rht,rthd->rhd", old_weight, value_heads, preferred_element_type=jnp.float32
    )
    context = context + own_weight.astype(jnp.float32)[:, :, None] * new_value.reshape(
        row_count, head_count, HD
    ).astype(jnp.float32)
    return context.reshape(row_count, head_count * HD).astype(jnp.bfloat16)


def attend_frames(queries, frames_kv, frame_counts):
    utterances = frame_counts.shape[0]
    beam_width = queries.shape[0] // utterances
    feature = queries.shape[1]
    head_count = feature // HD
    frame_total = frames_kv.shape[1]
    scale = HD ** (-0.5)
    query_heads = queries.reshape(utterances, beam_width, head_count, HD)
    key_heads = frames_kv[:, :, :feature].reshape(utterances, frame_total, head_count, HD)
    value_heads = frames_kv[:, :, feature:].reshape(utterances, frame_total, head_count, HD)
    scores = (
        jnp.einsum("ubhd,ufhd->uhbf", query_heads, key_heads, preferred_element_type=jnp.float32)
        * scale
    )
    live = (
        lax.broadcasted_iota(jnp.int32, (utterances, 1, 1, frame_total), 3)
        < frame_counts[:, None, None, None]
    )
    scores = jnp.where(live, scores, -1e30)
    peak = jnp.max(scores, axis=3, keepdims=True)
    raised = jnp.where(live, jnp.exp(scores - peak), 0.0)
    weights = (raised / jnp.sum(raised, axis=3, keepdims=True)).astype(jnp.bfloat16)
    context = jnp.einsum(
        "uhbf,ufhd->ubhd", weights, value_heads, preferred_element_type=jnp.float32
    )
    return context.reshape(utterances * beam_width, feature)


def body(cache_kv, new_rows, cross_queries, enc_kv, lengths, parents):
    feature = cross_queries.shape[1]
    cross_context = attend_frames(cross_queries, enc_kv, lengths)
    arrived, new_here = (
        lax.all_to_all(cache_kv, "utt", split_axis=0, concat_axis=0, tiled=True),
        lax.all_to_all(new_rows, "utt", split_axis=0, concat_axis=0, tiled=True),
    )
    reordered = reorder(arrived, parents)
    self_context = attend_self(
        new_here[:, :feature],
        reordered[:, :, :feature],
        reordered[:, :, feature:],
        new_here[:, feature : 2 * feature],
        new_here[:, 2 * feature :],
    )
    mixed_here = (self_context.astype(jnp.float32) + cross_context).astype(jnp.bfloat16)
    mixed = lax.all_to_all(mixed_here, "utt", split_axis=0, concat_axis=0, tiled=True)
    return mixed


def solution(mesh):
    placed = (
        P(("groups", "utt"), None, None),
        P(("groups", "utt"), None),
        P(("groups", "utt"), None),
        P(("groups", "utt"), None, None),
        P(("groups", "utt")),
        P(("groups", "utt"), None),
    )
    n = mesh.shape["utt"]

    def either(cache_kv, new_rows, cross_queries, enc_kv, lengths, parents):
        feature = cross_queries.shape[1]
        fits = (
            parents.shape == (1, n)
            and cache_kv.shape[0] == n
            and n % TEAM == 0
            and n > TEAM
            and feature % (TEAM * HD) == 0
            and cache_kv.shape[0] * cache_kv.shape[1] == HD
            and feature // (TEAM * HD) * n <= HD
        )
        run = functools.partial(fast_body, n) if fits else body
        return run(cache_kv, new_rows, cross_queries, enc_kv, lengths, parents)

    return jax.shard_map(
        either, mesh=mesh, in_specs=placed, out_specs=P(("groups", "utt"), None), check_vma=False
    )
```
